128 devices in a mesh: req: 16 (over z, x), kv: 8 (over y, core).
Axes of the slice: x: 4, y: 4, z: 4, core: 2. Of those that a mesh axis runs over, the one named last changes fastest.
Arguments:
- hidden_in: bfloat16 [2048, 1536], P('req'), may hold values from -6 to 6
- attn_gain: float32 [1536], replicated, may hold values from 0.1 to 1.9
- w_query: bfloat16 [1536, 1536], P('kv'), may hold values from -0.15625 to 0.15625
- w_key: bfloat16 [512, 1536], P('kv'), may hold values from -0.15625 to 0.15625
- w_value: bfloat16 [512, 1536], P('kv'), may hold values from -0.15625 to 0.15625
- w_out: bfloat16 [1536, 1536], P('kv'), may hold values from -0.75 to 0.75
- k_cache: bfloat16 [6144, 8, 8192], P('req', 'kv'), may hold values from -600 to 600
- v_cache: bfloat16 [6144, 8, 8192], P('req', 'kv'), may hold values from -6 to 6
- cache_len: int32 [2048], replicated, may hold values from 1 to 384, 393216 in all
- block_slot: int32 [6144], P('req'), may hold values from 0 to 6143, as said below
- moe_gain: float32 [1536], replicated, may hold values from 0.1 to 1.9
- w_router: bfloat16 [1536, 32], replicated, may hold values from -0.15625 to 0.15625
- w_gate_up: bfloat16 [32, 1536, 1024], P('req'), may hold values from -0.15625 to 0.15625
- w_down: bfloat16 [32, 512, 1536], P('req'), may hold values from -0.25 to 0.25
- routes: int32 [2048, 8], P(('req', 'kv')), may hold values from 0 to 31, all different within a row; in each aligned block of 16 rows (0 to 15, 16 to 31, ...) at most 16 rows name the same one
Outputs:
- layer_out: bfloat16 [2048, 1536], P(('req', 'kv'))
The draws below stay inside these ranges and needn't reach their ends.
Inputs may be any that keep to these rules, and one draw needn't show every extreme that they name: `block_slot`: each value once; the block holds page v % 3 of request v // 3; the blocks of one index of req hold exactly 128 * 3 / 16 pages of the requests of each index of req. `routes`: each row names 8 different experts; in the 16 rows of one device an expert may be named by all of them.
All inputs are finite; a program needn't handle non-finite values.
Results may differ from the reference program's by a relative error of at most 0.02.
The reference program's roundings to bfloat16 on the way (of `normed`, `query`, `key_new`, `value_new`, `attended`, `moe_in`, `activated` and `expert_out`) count: a program that leaves them out, or rounds other values in their place, can miss the bound.
Values may be sent and summed in bfloat16 or wider, within the bound.
A program may use at most 192 MiB of HBM per device.

```python
import math
import jax
import jax.numpy as jnp
import numpy as np
from jax import lax

D = 1536
HEADS = 24
KVH = 8
HD = 64
FFE = 512
TOPK = 8
R_DEV = 128
MAXLEN = 384
BLK = 128
PAGES = 3
REQUESTS = 2048
NBLOCKS = 6144
TOK_DEV = 16
EXPERTS = 32
N_REQ = 16


def draw_k_cache(key, part):
    first = jax.random.fold_in(key, 0)
    base = jnp.clip(jax.random.normal(first, (NBLOCKS, KVH, BLK, HD), jnp.float32), -4.0, 4.0)
    return base.reshape(NBLOCKS, KVH, BLK * HD).astype(jnp.bfloat16)


def draw_block_slot(key, part):
    per_home = R_DEV * PAGES
    share = per_home // N_REQ
    first, second = jax.random.split(jax.random.fold_in(key, 17))
    home_keys = jax.random.split(first, N_REQ)
    home_perms = jax.vmap(lambda k: jax.random.permutation(k, per_home))(home_keys).astype(jnp.int32)
    device_ids = jnp.arange(N_REQ, dtype=jnp.int32)[:, None]
    slot_ids = jnp.arange(per_home, dtype=jnp.int32)[None, :]
    home_ids = slot_ids // share
    picked = home_perms[home_ids, device_ids * share + slot_ids % share]
    values = (home_ids * per_home + picked).astype(jnp.int32)
    shuffle_keys = jax.random.split(second, N_REQ)
    shuffles = jax.vmap(lambda k: jax.random.permutation(k, per_home))(shuffle_keys).astype(jnp.int32)
    values = jnp.take_along_axis(values, shuffles, 1)
    return values.reshape(-1).astype(jnp.int32)


def levels(rng, shape, shards, least, largest):
    def one(position, shards_of):
        steps = jax.random.uniform(jax.random.fold_in(jax.random.fold_in(rng, 6), position), (shards_of,), jnp.float32, least / len(shards), largest / len(shards))
        return jnp.repeat(jnp.exp(steps), shape[position] // shards_of).reshape((-1,) + (1,) * (len(shape) - position - 1))

    level = one(*shards[0])
    for cut in shards[1:]:
        level = level * one(*cut)
    return level


def split_up(number_of, total, bound, lean):
    weights = [(1 << 20) // math.isqrt(rank ** lean) + 1 for rank in range(2, number_of + 1)]
    rest, holding = total - bound - (number_of - 1), [1] * (number_of - 1)
    while rest > 0:
        free = [i for i in range(number_of - 1) if holding[i] < bound]
        mass, left = sum([weights[i] for i in free]), rest
        for i in free:
            addition = min(bound - holding[i], max(1, left * weights[i] // mass), rest)
            holding[i] = holding[i] + addition
            rest = rest - addition
    return np.array([bound] + holding)


def uneven(stream_key, amount, total, bound, lean):
    if amount == 2:
        one = jax.random.randint(stream_key, (), max(1, total - bound), min(bound, total - 1) + 1)
        return jnp.stack([one, total - one])
    lengths = jnp.asarray(split_up(amount, total, bound, lean), jnp.int32)
    couples = (amount - 1) // 2
    giver, receiver = lengths[1:1 + 2 * couples:2], lengths[2:2 + 2 * couples:2]
    room = jnp.minimum(giver - 1, bound - receiver)
    passed = jax.random.randint(jax.random.fold_in(stream_key, 1), (couples,), 0, 1 << 20) % (room + 1)
    lengths = lengths.at[1:1 + 2 * couples:2].set(giver - passed).at[2:2 + 2 * couples:2].set(receiver + passed)
    return lengths[jax.random.permutation(jax.random.fold_in(stream_key, 2), amount)]


def routed_block(key, own, number, rows, count, top, limit, lean):
    sequence = jax.random.permutation(key, count)
    heavy_load, usual = portions_of(count, rows * top, limit, lean, True), portions_of(count, rows * top, limit, lean, False)
    places = jnp.arange(count)

    def named(tallies, turn):
        used = int((tallies > 0).sum())
        fixed = max(1, used // 4)
        moved = fixed + (places - fixed + turn * (used - fixed)) % max(1, count - fixed)
        return jnp.zeros((count,), jnp.int32).at[sequence[jnp.where(places < fixed, places, moved)]].set(jnp.asarray(tallies, jnp.int32))

    tallies = jnp.where(number % 4 == 0, named(heavy_load, number // 4), named(usual, number - number // 4 - 1))
    mixed = jax.random.permutation(jax.random.fold_in(own, 3), count)
    donor, taker = mixed[0:count // 2 * 2:2], mixed[1:count // 2 * 2:2]
    margin = jnp.minimum(tallies[donor] - 1, limit - tallies[taker]) // 2
    margin = jnp.where((donor == sequence[0]) | (taker == sequence[0]) | (tallies[taker] == 0), 0, jnp.maximum(margin, 0))
    moved = jax.random.randint(jax.random.fold_in(own, 4), (count // 2,), 0, 1 << 20) % (margin + 1)
    tallies = tallies.at[donor].add(-moved).at[taker].add(moved)
    labels = jnp.searchsorted(jnp.cumsum(tallies), jnp.arange(rows * top), side="right").astype(jnp.int32)
    table = labels.reshape(top, rows).T
    table = table[jax.random.permutation(jax.random.fold_in(own, 1), rows)]
    turn = jax.random.randint(jax.random.fold_in(own, 2), (rows, 1), 0, top)
    return jnp.take_along_axis(table, (jnp.arange(top)[None, :] + turn) % top, axis=1)


def portions_of(number_of, total, limit, lean, full):
    weights = [(1 << 20) // math.isqrt(standing ** lean) + 1 for standing in range(1, number_of + 1)]
    largest = limit if full else min(limit, max(-(-total // number_of), total * weights[0] // sum(weights)))
    least = 1 if total - largest >= number_of - 1 else 0
    counts, rest = [largest] + [least] * (number_of - 1), total - largest - least * (number_of - 1)
    while rest > 0:
        movable = [i for i in range(1, number_of) if counts[i] < largest] or [i for i in range(1, number_of) if counts[i] < limit]
        whole, budget = sum([weights[i] for i in movable]), rest
        for i in movable:
            extra = min(limit - counts[i], max(1, budget * weights[i] // whole), rest)
            counts[i] = counts[i] + extra
            rest = rest - extra
    return np.array(counts)


def gaussian(rng, dims, width, limit, shards=(), kind=jnp.bfloat16):
    level = levels(rng, dims, shards, -0.22, 0.18) if shards else 1.0
    drawn = jax.random.normal(rng, dims, jnp.float32) * width * level
    return jnp.minimum(jnp.maximum(drawn, -limit), limit).astype(kind)


def setup_inputs(seed: int = 0) -> dict:
    splits = jax.random.split(jax.random.key(seed), 16)
    hidden_in = gaussian(splits[0], (REQUESTS, D), 1.0, 6.0, ((0, 16),))
    attn_gain = jnp.clip(1.0 + 0.18 * jax.random.normal(splits[1], (D,), jnp.float32), 0.1, 1.9)
    w_query = gaussian(splits[2], (HEADS * HD, D), D ** -0.5, 0.15625, ((0, 8),))
    w_key = gaussian(splits[3], (KVH * HD, D), D ** -0.5, 0.15625, ((0, 8),))
    w_value = gaussian(splits[4], (KVH * HD, D), D ** -0.5, 0.15625, ((0, 8),))
    w_out = gaussian(splits[5], (HEADS * HD, D), HD ** -0.5, 0.75, ((0, 8),))
    k_cache = draw_k_cache(jax.random.fold_in(splits[15], 71), 0)
    v_cache = gaussian(splits[7], (NBLOCKS, KVH, BLK * HD), 1.0, 6.0, ((0, 16), (1, 8)))
    cache_len = uneven(splits[8], REQUESTS, REQUESTS * MAXLEN // 2, MAXLEN, 2).astype(jnp.int32)
    block_slot = draw_block_slot(jax.random.fold_in(splits[15], 71), 0)
    moe_gain = jnp.clip(1.0 + 0.18 * jax.random.normal(splits[10], (D,), jnp.float32), 0.1, 1.9)
    w_router = gaussian(splits[11], (D, EXPERTS), D ** -0.5, 0.15625)
    w_gate_up = gaussian(splits[12], (EXPERTS, D, 2 * FFE), D ** -0.5, 0.15625, ((0, 16),))
    w_down = gaussian(splits[13], (EXPERTS, FFE, D), FFE ** -0.5, 0.25, ((0, 16),))
    routes_keys = jax.random.split(jax.random.fold_in(splits[14], 1), REQUESTS // TOK_DEV)
    routes_turns = jax.random.permutation(jax.random.fold_in(splits[14], 3), REQUESTS // TOK_DEV)
    routes = jax.vmap(lambda own, number: routed_block(jax.random.fold_in(splits[14], 2), own, number, TOK_DEV, EXPERTS, TOPK, TOK_DEV, 2))(routes_keys, routes_turns).reshape((REQUESTS, TOPK))
    return {"hidden_in": hidden_in, "attn_gain": attn_gain, "w_query": w_query, "w_key": w_key, "w_value": w_value, "w_out": w_out, "k_cache": k_cache, "v_cache": v_cache, "cache_len": cache_len, "block_slot": block_slot, "moe_gain": moe_gain, "w_router": w_router, "w_gate_up": w_gate_up, "w_down": w_down, "routes": routes}


def rms_norm(values, gain):
    values = values.astype(jnp.float32)
    return values * lax.rsqrt(lax.optimization_barrier(jnp.mean(values * values, -1, keepdims=True)) + 1e-05) * gain

def rotate(values, positions):
    half_dim = values.shape[-1] // 2
    frequency = 10000.0 ** (-jnp.arange(half_dim, dtype=jnp.float32) / half_dim)
    angles = positions.astype(jnp.float32)[:, None, None] * frequency
    cosines = jnp.cos(angles)
    sines = jnp.sin(angles)
    first_half = values[..., :half_dim]
    second_half = values[..., half_dim:]
    return jnp.concatenate([first_half * cosines - second_half * sines, first_half * sines + second_half * cosines], -1)

def project_rows(normed, weight):
    return lax.dot_general(normed, weight, (((1,), (1,)), ((), ())), preferred_element_type=jnp.float32)

def by_position(blocks_data):
    return blocks_data.reshape(R_DEV, PAGES, KVH, BLK, HD).transpose(0, 1, 3, 2, 4).reshape(R_DEV, MAXLEN, KVH, HD)

def reference(hidden_in, attn_gain, w_query, w_key, w_value, w_out, k_cache, v_cache, cache_len, block_slot, moe_gain, w_router, w_gate_up, w_down, routes):
    request_count = hidden_in.shape[0]
    normed = rms_norm(hidden_in, attn_gain).astype(jnp.bfloat16)
    query = project_rows(normed, w_query).reshape(request_count, HEADS, HD)
    query = (rotate(query, cache_len) * 0.125).astype(jnp.bfloat16)
    key_new = project_rows(normed, w_key).reshape(request_count, KVH, HD)
    key_new = rotate(key_new, cache_len).astype(jnp.bfloat16)
    value_new = project_rows(normed, w_value).astype(jnp.bfloat16).reshape(request_count, KVH, HD)
    block_of_slot = jnp.argsort(block_slot).astype(jnp.int32)
    positions = jnp.arange(MAXLEN, dtype=jnp.int32)
    per_group = HEADS // KVH

    def attend(group_index):
        request_rows = group_index * R_DEV + jnp.arange(R_DEV, dtype=jnp.int32)
        slot_ids = request_rows[:, None] * PAGES + jnp.arange(PAGES, dtype=jnp.int32)[None, :]
        blocks = block_of_slot[slot_ids.reshape(-1)]
        cache_keys = by_position(k_cache[blocks]).astype(jnp.float32)
        cache_values = by_position(v_cache[blocks]).astype(jnp.float32)
        start = (group_index * R_DEV).astype(jnp.int32)
        query_group = lax.dynamic_slice_in_dim(query, start, R_DEV, 0).reshape(R_DEV, KVH, per_group, HD).astype(jnp.float32)
        newkey_group = lax.dynamic_slice_in_dim(key_new, start, R_DEV, 0).astype(jnp.float32)
        newvalue_group = lax.dynamic_slice_in_dim(value_new, start, R_DEV, 0).astype(jnp.float32)
        length_group = lax.dynamic_slice_in_dim(cache_len, start, R_DEV, 0)
        scores = jnp.einsum('rgqd,rtgd->rgqt', query_group, cache_keys, precision=lax.Precision.HIGHEST)
        usable = positions[None, :] < length_group[:, None]
        scores = jnp.where(usable[:, None, None, :], scores, -jnp.inf)
        own_score = jnp.einsum('rgqd,rgd->rgq', query_group, newkey_group, precision=lax.Precision.HIGHEST)
        highest = jnp.maximum(lax.optimization_barrier(jnp.max(scores, -1)), own_score)
        weights = jnp.exp(scores - highest[..., None])
        own_weight = jnp.exp(own_score - highest)
        total = lax.optimization_barrier(jnp.sum(weights, -1)) + own_weight
        numer = jnp.einsum('rgqt,rtgd->rgqd', weights, cache_values, precision=lax.Precision.HIGHEST)
        numer = numer + own_weight[..., None] * newvalue_group[:, :, None, :]
        return (numer / total[..., None]).reshape(R_DEV, HEADS * HD)
    attended = lax.map(attend, jnp.arange(N_REQ, dtype=jnp.int32)).reshape(request_count, HEADS * HD).astype(jnp.bfloat16)
    after_attn = hidden_in.astype(jnp.float32) + jnp.dot(attended, w_out, preferred_element_type=jnp.float32)
    moe_in = rms_norm(after_attn, moe_gain).astype(jnp.bfloat16)
    logits = jnp.dot(moe_in, w_router, preferred_element_type=jnp.float32)
    chosen = jnp.take_along_axis(logits, routes, 1)
    gate_probs = jax.nn.softmax(chosen, -1)
    flat_expert = routes.reshape(-1)
    order = jnp.argsort(flat_expert).astype(jnp.int32)
    token_of = (order // TOPK).astype(jnp.int32)
    expert_count = w_router.shape[1]
    group_sizes = lax.optimization_barrier(jnp.sum((flat_expert[:, None] == jnp.arange(expert_count, dtype=jnp.int32)[None, :]).astype(jnp.int32), 0)).astype(jnp.int32)
    expert_in = moe_in[token_of]
    gate_up = lax.ragged_dot(expert_in, w_gate_up, group_sizes, preferred_element_type=jnp.float32)
    activated = (jax.nn.silu(gate_up[:, :FFE]) * gate_up[:, FFE:]).astype(jnp.bfloat16)
    expert_out = lax.ragged_dot(activated, w_down, group_sizes, preferred_element_type=jnp.float32).astype(jnp.bfloat16)
    weight = gate_probs.reshape(-1)[order]
    mixture = jax.ops.segment_sum(expert_out.astype(jnp.float32) * weight[:, None], token_of, num_segments=request_count)
    return (after_attn + mixture).astype(jnp.bfloat16)
```

```python
import jax
import jax.numpy as jnp
from jax import lax
from jax.experimental import pallas as pl
from jax.experimental.pallas import tpu as pltpu
from jax.sharding import PartitionSpec as P

HD = 64
FFE = 512
BLK = 128
PAGES = 3
PAD = 32
LOW = -1e30
MESH = pl.DeviceIdType.MESH
F32 = jnp.float32
BF16 = jnp.bfloat16


def dot_nt(left, right):
    return lax.dot_general(left, right, (((1,), (1,)), ((), ())), preferred_element_type=F32)


def dot_nn(left, right):
    return jnp.dot(left, right, preferred_element_type=F32)


def iota(shape, axis):
    return lax.broadcasted_iota(jnp.int32, shape, axis)


def split_3(value):
    high = value.astype(BF16).astype(F32)
    rest = value - high
    middle = rest.astype(BF16).astype(F32)
    return high, middle, rest - middle


def kernel(
    hidden_hbm, gain_ref, wq_hbm, wk_hbm, wv_hbm, wout_hbm, k_hbm, v_hbm, lens_ref, slots_ref,
    moe_gain_ref, router_ref, up_hbm, down_hbm, routes_ref,
    out_ref,
    hid, wqkv, wout, kbuf, vbuf, up, down,
    pm_send, pm_recv, q_send, q_recv, q6, thr, part, part_send, part_recv, gather_t,
    rotated, value_new, proj, proj_recv, tok_send, tok, act, mixed, mixed_send, mixed_recv,
    local_sem, send_sem, recv_sem,
):
    me = lax.axis_index("req")
    kv = lax.axis_index("kv")
    mz, mx = me // 4, me % 4
    n_req, n_kv = 16, 8
    rows, model = hid.shape
    blocks = kbuf.shape[0]

    loads = [
        (hidden_hbm, hid), (wq_hbm, wqkv.at[pl.ds(0, 192)]), (wk_hbm, wqkv.at[pl.ds(192, 64)]),
        (wv_hbm, wqkv.at[pl.ds(256, 64)]), (k_hbm, kbuf), (v_hbm, vbuf), (wout_hbm, wout),
        (up_hbm, up), (down_hbm, down),
    ]
    loads = [
        pltpu.make_async_copy(src, dst, local_sem.at[i]) for i, (src, dst) in enumerate(loads)
    ]
    for load in loads:
        load.start()

    def req_peer(o):
        return ((mz + o // 4) % 4) * 4 + (mx + o % 4) % 4

    def kv_peer(o):
        return (kv + o) % n_kv

    barrier = pltpu.get_barrier_semaphore()

    def greet_req(o, carry):
        pl.semaphore_signal(barrier, inc=1, device_id={"req": req_peer(o)}, device_id_type=MESH)
        return carry

    def greet_kv(o, carry):
        pl.semaphore_signal(barrier, inc=1, device_id={"kv": kv_peer(o)}, device_id_type=MESH)
        return carry

    lax.fori_loop(1, n_req, greet_req, 0)
    lax.fori_loop(1, n_kv, greet_kv, 0)

    def remote(phase, o, axis, source, target):
        peer = req_peer(o) if axis == "req" else kv_peer(o)
        return pltpu.make_async_remote_copy(
            src_ref=source(peer), dst_ref=target, send_sem=send_sem.at[phase, o],
            recv_sem=recv_sem.at[phase, o], device_id={axis: peer}, device_id_type=MESH,
        )

    def start_all(phase, count, axis, source, target):
        def body(o, carry):
            remote(phase, o, axis, source, target).start()
            return carry

        lax.fori_loop(1, count, body, 0)

    def wait_recv_all(phase, count, axis, source, target):
        def body(o, carry):
            remote(phase, o, axis, source, target).wait_recv()
            return carry

        lax.fori_loop(1, count, body, 0)

    def wait_send_all(phase, count, axis, source, target):
        def body(o, carry):
            remote(phase, o, axis, source, target).wait_send()
            return carry

        lax.fori_loop(1, count, body, 0)

    eye = iota((128, 128), 0) == iota((128, 128), 1)

    def column(row):
        return jnp.sum(jnp.where(eye, row, 0.0), 1, keepdims=True)

    slots = slots_ref[...]
    owner = (slots * 43691) >> 17
    page = slots - owner * PAGES
    home = owner >> 7
    place = page * 128 + (owner & 127)
    home_f = home.astype(F32)
    place_f = place.astype(F32)
    home_row = jnp.concatenate([home_f[i : i + 1] for i in range(3)], 1)
    place_row = jnp.concatenate([place_f[i : i + 1] for i in range(3)], 1)
    home_col = jnp.concatenate([column(home_f[i : i + 1]) for i in range(3)], 0)
    place_col = jnp.concatenate([column(place_f[i : i + 1]) for i in range(3)], 0)
    home_hot = (home_row == iota((16, blocks), 0).astype(F32)).astype(F32).astype(BF16)
    place_hot = (place_col == iota((blocks, blocks), 1).astype(F32)).astype(F32).astype(BF16)
    present = dot_nn(home_hot, place_hot)
    pm_send[...] = jnp.zeros_like(pm_send)
    for j in range(PAGES):
        pm_send[:, j, :] = present[:, 128 * j : 128 * (j + 1)]

    pl.semaphore_wait(barrier, n_req + n_kv - 2)
    presence = (0, n_req, "req", lambda peer: pm_send.at[peer], pm_recv.at[me])
    start_all(*presence)
    pm_recv[pl.ds(me, 1)] = pm_send[pl.ds(me, 1)]

    order_row = home_row * 384.0 + place_row
    order_col = home_col * 384.0 + place_col
    before = (order_col < order_row).astype(F32)
    slot_row = jnp.sum(before, 0, keepdims=True) + 8.0 * home_row
    after = (order_row < order_col).astype(F32)
    slot_col = jnp.sum(after, 1, keepdims=True) + 8.0 * home_col
    n_slot = n_req * PAD

    len_row = lens_ref[pl.ds(me, 1), :].astype(F32)
    len_col = column(len_row)
    lane = iota((rows, 256), 1)
    frequency = jnp.exp((lane & 31).astype(F32) * (-9.210340371976184 / 32.0))
    angles = len_col * frequency
    cosines = jnp.cos(angles)
    sines = jnp.sin(angles)
    upper = (lane & 63) >= 32
    for load in loads[:4]:
        load.wait()
    values = hid[...].astype(F32)
    scale = lax.rsqrt(jnp.mean(values * values, -1, keepdims=True) + 1e-05)
    normed = (values * scale * gain_ref[...]).astype(BF16)
    qk = dot_nt(normed, wqkv[pl.ds(0, 256), :])
    value_new[...] = dot_nt(normed, wqkv[pl.ds(256, 64), :]).astype(BF16)
    swapped = jnp.where(upper, pltpu.roll(qk, 32, 1), pltpu.roll(qk, 224, 1))
    turned = qk * cosines + jnp.where(upper, swapped, -swapped) * sines
    turned = jnp.where(lane < 192, turned * 0.125, turned).astype(BF16)
    rotated[...] = turned

    wait_recv_all(*presence)
    held = pm_recv[...].reshape(128, 128)
    held_b = held.astype(BF16)
    r0, c0 = iota((128, 128), 0), iota((128, 128), 1)
    ahead = (r0 < c0).astype(F32).astype(BF16)
    earlier = (((r0 >> 3) == (c0 >> 3)) & (c0 < r0)).astype(F32).astype(BF16)
    ones = jnp.ones((128, 128), BF16)
    counts = dot_nn(held_b, ahead) + dot_nn(dot_nn(earlier, held_b).astype(BF16), ones)
    source_slot = held * (counts + ((r0 >> 3) * PAD).astype(F32))
    page_slot = jnp.sum(source_slot.reshape(16, 8, 128), 0)
    page_row = jnp.concatenate([page_slot[j : j + 1] for j in range(PAGES)], 1)
    page_col = jnp.concatenate([column(page_slot[j : j + 1]) for j in range(PAGES)], 0)
    pick = (iota((n_slot, blocks), 0).astype(F32) == page_row).astype(F32).astype(BF16)
    gather_t[...] = (iota((blocks, n_slot), 1).astype(F32) == page_col).astype(F32).astype(BF16)
    extended = []
    for j in range(PAGES):
        used = jnp.clip(len_col - 128.0 * j, 0.0, 128.0)
        extended.append(jnp.where(lane < 192, turned.astype(F32), used).astype(BF16))
    q_send[...] = dot_nn(pick, jnp.concatenate(extended, 0)).astype(BF16)

    def slot_rows(index):
        return pl.ds(pl.multiple_of(index * PAD, PAD), PAD)

    queries = (1, n_req, "req", lambda peer: q_send.at[slot_rows(peer)], q_recv.at[slot_rows(me)])
    start_all(*queries)
    q_recv[slot_rows(me), :] = q_send[slot_rows(me), :]
    place_slot = (slot_col == iota((blocks, n_slot), 1).astype(F32)).astype(F32).astype(BF16)
    wait_recv_all(*queries)
    arrived = dot_nn(place_slot, q_recv[...])
    zeros = jnp.zeros((blocks, HD), BF16)
    for q in range(3):
        head = arrived[:, HD * q : HD * (q + 1)].astype(BF16)
        q6[q] = jnp.concatenate([head, zeros], 1)
        q6[q + 3] = jnp.concatenate([zeros, head], 1)
    limit = arrived[:, 192:256]
    thr[...] = jnp.concatenate([limit, limit], 1)

    loads[4].wait()
    loads[5].wait()
    wide_r, wide_c = iota((96, 256), 0), iota((96, 256), 1)
    position = jnp.where((wide_r & 15) == (wide_c & 15), 2 * (wide_c >> 4), 1 << 20).astype(F32)
    stat_lane = iota((16, HD), 1)

    def one_group(g):
        here = pl.ds(pl.multiple_of(g * 16, 16), 16)
        query = q6[:, here, :].reshape(96, 128)
        bound = thr[here, :]
        bound = jnp.concatenate([bound] * 3 + [bound - 1.0] * 3, 0)
        bound = jnp.concatenate([bound, bound], 1)
        scores = []
        for c in range(4):
            keys = jnp.concatenate(
                [kbuf[here, 128 * i : 128 * (i + 1)] for i in range(16 * c, 16 * c + 16)], 0
            )
            scores.append(jnp.where(position < bound - 32.0 * c, dot_nt(query, keys), LOW))
        top = jnp.maximum(jnp.maximum(scores[0], scores[1]), jnp.maximum(scores[2], scores[3]))
        top = jnp.max(top, 1, keepdims=True)
        top = jnp.maximum(jnp.maximum(top[:48], top[48:]), -1e29)
        top_2 = jnp.concatenate([top, top], 0)
        weights = [jnp.exp(s - top_2) for s in scores]
        total = jnp.sum((weights[0] + weights[1]) + (weights[2] + weights[3]), 1, keepdims=True)
        total = total[:48] + total[48:]
        numer = jnp.zeros((96, 128), F32)
        for c in range(4):
            vals = jnp.concatenate(
                [vbuf[here, 128 * i : 128 * (i + 1)] for i in range(16 * c, 16 * c + 16)], 0
            )
            numer = numer + dot_nn(weights[c].astype(BF16), vals)
        numer = numer[:48, :HD] + numer[48:, HD:]
        some = total > 0.0
        safe = jnp.where(some, total, 1.0)
        numer = numer / safe
        lse = jnp.where(some, top + jnp.log(safe), LOW)
        pieces = [numer[16 * q : 16 * (q + 1)] for q in range(3)]
        stats = jnp.zeros((16, HD), F32)
        for q in range(3):
            for t, term in enumerate(split_3(lse[16 * q : 16 * (q + 1)])):
                stats = jnp.where(stat_lane == 16 * t + q, term, stats)
        part[here, :] = jnp.concatenate(pieces + [stats], 1).astype(BF16)

    def group_step(step, carry):
        for k in range(2):
            one_group(step * 2 + k)
        return carry

    lax.fori_loop(0, blocks // 32, group_step, 0)

    slot_place = (iota((n_slot, blocks), 0).astype(F32) == slot_row).astype(F32).astype(BF16)
    part_send[...] = dot_nn(slot_place, part[...]).astype(BF16)
    partials = (
        2, n_req, "req", lambda peer: part_send.at[slot_rows(peer)], part_recv.at[slot_rows(me)],
    )
    start_all(*partials)
    part_recv[slot_rows(me), :] = part_send[slot_rows(me), :]
    own_q = rotated[...].astype(F32)
    own_k = own_q[:, 192:256]
    own_v = value_new[...].astype(F32)
    own_score = [
        jnp.sum(own_q[:, HD * q : HD * (q + 1)] * own_k, 1, keepdims=True) for q in range(3)
    ]
    wait_recv_all(*partials)
    pages = dot_nn(gather_t[...], part_recv[...])
    attended = []
    for q in range(3):
        lses, outs = [own_score[q]], [own_v]
        for j in range(PAGES):
            piece = pages[128 * j : 128 * (j + 1)]
            lses.append(
                piece[:, 192 + q : 193 + q]
                + piece[:, 208 + q : 209 + q]
                + piece[:, 224 + q : 225 + q]
            )
            outs.append(piece[:, HD * q : HD * (q + 1)])
        peak = jnp.maximum(jnp.maximum(lses[0], lses[1]), jnp.maximum(lses[2], lses[3]))
        shares = [jnp.exp(value - peak) for value in lses]
        whole = (shares[0] + shares[1]) + (shares[2] + shares[3])
        summed = shares[0] * outs[0] + shares[1] * outs[1]
        summed = summed + shares[2] * outs[2] + shares[3] * outs[3]
        attended.append((summed / whole).astype(BF16))
    attended = jnp.concatenate(attended, 1)

    loads[6].wait()
    for n in range(0, model, 512):
        proj[:, n : n + 512] = dot_nn(attended, wout[:, n : n + 512]).astype(BF16)

    def token_rows(index):
        return pl.ds(pl.multiple_of(index * 16, 16), 16)

    sums = (3, n_kv, "kv", lambda peer: proj.at[token_rows(peer)], proj_recv.at[kv])
    start_all(*sums)
    proj_recv[pl.ds(kv, 1)] = proj[token_rows(kv), :].reshape(1, 16, model)
    expert_lane = iota((16, 128), 1)
    chosen = jnp.zeros((16, 128), F32)
    for k in range(8):
        chosen = chosen + (routes_ref[:, k : k + 1] == expert_lane).astype(F32)
    wait_recv_all(*sums)
    after_attn = hid[token_rows(kv), :].astype(F32)
    total = proj_recv[0].astype(F32)
    for k in range(1, n_kv):
        total = total + proj_recv[k].astype(F32)
    after_attn = after_attn + total
    scale = lax.rsqrt(jnp.mean(after_attn * after_attn, -1, keepdims=True) + 1e-05)
    moe_in = (after_attn * scale * moe_gain_ref[...]).astype(BF16)
    logits = dot_nt(moe_in, router_ref[...])
    logits = jnp.concatenate([logits] * 4, 1)
    logits = jnp.where(chosen > 0.0, logits, LOW)
    gates = jnp.exp(logits - jnp.max(logits, 1, keepdims=True))
    gates = gates / jnp.sum(gates, 1, keepdims=True)
    high, middle, low = split_3(gates)
    tok_send[:, :model] = moe_in
    tok_send[:, model:] = jnp.concatenate(
        [high[:, :32], middle[:, :32], low[:, :32], jnp.zeros((16, 32), F32)], 1
    ).astype(BF16)

    tokens = (4, n_req, "req", lambda peer: tok_send, tok.at[token_rows(me)])
    start_all(*tokens)
    tok[token_rows(me), :] = tok_send[...]
    loads[7].wait()
    loads[8].wait()
    wait_recv_all(*tokens)
    gate_all = tok[:, model:].astype(F32)
    gate_lane = iota((256, 128), 1)
    for e in range(2):
        def up_step(f, carry):
            at_gate = pl.ds(pl.multiple_of(f * 256, 256), 256)
            at_up = pl.ds(pl.multiple_of(FFE + f * 256, 256), 256)
            gate = dot_nn(tok[:, :model], up[e, :, at_gate])
            lift = dot_nn(tok[:, :model], up[e, :, at_up])
            act[:, at_gate] = (gate * jax.nn.sigmoid(gate) * lift).astype(BF16)
            return carry

        lax.fori_loop(0, 2, up_step, 0)
        index = 2 * me + e
        mine = ((gate_lane & 31) == index) & (gate_lane < 96)
        weight = jnp.sum(jnp.where(mine, gate_all, 0.0), 1, keepdims=True)

        def down_step(n, carry):
            here = pl.ds(pl.multiple_of(n * 256, 256), 256)
            made = dot_nn(act[...], down[e, :, here]).astype(BF16).astype(F32) * weight
            if e == 0:
                mixed[:, here] = made
            else:
                mixed_send[:, here] = (mixed[:, here] + made).astype(BF16)
            return carry

        lax.fori_loop(0, model // 256, down_step, 0)
    backs = (
        5, n_req, "req", lambda peer: mixed_send.at[token_rows(peer)], mixed_recv.at[me],
    )
    start_all(*backs)
    mixed_recv[pl.ds(me, 1)] = mixed_send[token_rows(me), :].reshape(1, 16, model)
    wait_recv_all(*backs)
    result = mixed_recv[0].astype(F32)
    for d in range(1, n_req):
        result = result + mixed_recv[d].astype(F32)
    out_ref[...] = (after_attn + result).astype(BF16)
    for exchange in (presence, queries, partials, sums, tokens, backs):
        wait_send_all(*exchange)


def shards(
    hidden_in, attn_gain, w_query, w_key, w_value, w_out, k_cache, v_cache, cache_len, block_slot,
    moe_gain, w_router, w_gate_up, w_down, routes,
):
    any_spec = pl.BlockSpec(memory_space=pl.ANY)
    vmem = pl.BlockSpec(memory_space=pltpu.VMEM)
    blocks = k_cache.shape[0]
    model = hidden_in.shape[1]
    rows = hidden_in.shape[0]
    n_slot = 16 * PAD
    scratch = [
        ((rows, model), BF16), ((320, model), BF16), ((192, model), BF16),
        ((blocks, 8192), BF16), ((blocks, 8192), BF16),
        (w_gate_up.shape, BF16), (w_down.shape, BF16),
        ((16, 8, 128), F32), ((16, 8, 128), F32),
        ((n_slot, 256), BF16), ((n_slot, 256), BF16),
        ((6, blocks, 128), BF16), ((blocks, 128), F32),
        ((blocks, 256), BF16), ((n_slot, 256), BF16), ((n_slot, 256), BF16),
        ((blocks, n_slot), BF16),
        ((rows, 256), BF16), ((rows, HD), BF16), ((rows, model), BF16), ((8, 16, model), BF16),
        ((16, model + 128), BF16), ((256, model + 128), BF16),
        ((256, FFE), BF16), ((256, model), F32), ((256, model), BF16), ((16, 16, model), BF16),
    ]
    return pl.pallas_call(
        kernel,
        out_shape=jax.ShapeDtypeStruct((16, model), BF16),
        in_specs=[
            any_spec, vmem, any_spec, any_spec, any_spec, any_spec, any_spec, any_spec, vmem, vmem,
            vmem, vmem, any_spec, any_spec, vmem,
        ],
        out_specs=vmem,
        scratch_shapes=[pltpu.VMEM(shape, dtype) for shape, dtype in scratch]
        + [
            pltpu.SemaphoreType.DMA((9,)),
            pltpu.SemaphoreType.DMA((6, 16)),
            pltpu.SemaphoreType.DMA((6, 16)),
        ],
        compiler_params=pltpu.CompilerParams(
            collective_id=0, has_side_effects=True, vmem_limit_bytes=56 << 20
        ),
    )(
        hidden_in, attn_gain.reshape(1, model), w_query, w_key, w_value, w_out,
        k_cache.reshape(blocks, 8192), v_cache.reshape(blocks, 8192),
        cache_len.reshape(16, 128), block_slot.reshape(3, 128),
        moe_gain.reshape(1, model), w_router.T, w_gate_up, w_down, routes,
    )


def solution(mesh):
    placed = (
        P("req", None),
        P(),
        P("kv", None),
        P("kv", None),
        P("kv", None),
        P("kv", None),
        P("req", "kv", None),
        P("req", "kv", None),
        P(),
        P("req"),
        P(),
        P(),
        P("req", None, None),
        P("req", None, None),
        P(("req", "kv"), None),
    )
    return jax.shard_map(
        shards, mesh=mesh, in_specs=placed, out_specs=P(("req", "kv"), None), check_vma=False
    )
```

```python
import jax
import jax.numpy as jnp
from jax import lax
from jax.experimental import pallas as pl
from jax.experimental.pallas import tpu as pltpu
from jax.sharding import PartitionSpec as P

HD = 64
FFE = 512
BLK = 128
PAGES = 3
PAD = 32
CHUNK = 64
LOW = -1e30
MESH = pl.DeviceIdType.MESH
F32 = jnp.float32
BF16 = jnp.bfloat16


def dot_nt(left, right):
    return lax.dot_general(left, right, (((1,), (1,)), ((), ())), preferred_element_type=F32)


def dot_nn(left, right):
    return jnp.dot(left, right, preferred_element_type=F32)


def iota(shape, axis):
    return lax.broadcasted_iota(jnp.int32, shape, axis)


def split_3(value):
    high = value.astype(BF16).astype(F32)
    rest = value - high
    middle = rest.astype(BF16).astype(F32)
    return high, middle, rest - middle


def kernel(
    hidden_hbm, gain_ref, wq_hbm, wk_hbm, wv_hbm, wout_hbm, k_hbm, v_hbm, lens_ref, slots_ref,
    moe_gain_ref, router_ref, up_hbm, down_hbm, routes_ref,
    out_ref,
    hid, wqkv, wout, kbuf, vbuf, up, down,
    pm_send, pm_recv, q_send, q_recv, q6, thr, part, part_send, part_recv, gather_t,
    rotated, value_new, proj, proj_recv, att, att_peer, wout_peer,
    tok_send, tok, mixed, mixed_send, mixed_recv,
    local_sem, send_sem, recv_sem,
):
    me = lax.axis_index("req")
    kv = lax.axis_index("kv")
    mz, mx = me // 4, me % 4
    n_req, n_kv = 16, 8
    rows, model = hid.shape
    blocks = kbuf.shape[0]

    loads = [
        (hidden_hbm, hid), (wq_hbm, wqkv.at[pl.ds(0, 192)]), (wk_hbm, wqkv.at[pl.ds(192, 64)]),
        (wv_hbm, wqkv.at[pl.ds(256, 64)]), (k_hbm, kbuf), (v_hbm, vbuf), (wout_hbm, wout),
        (up_hbm, up), (down_hbm, down),
    ]
    loads = [
        pltpu.make_async_copy(src, dst, local_sem.at[i]) for i, (src, dst) in enumerate(loads)
    ]
    for load in loads:
        load.start()

    def req_peer(o):
        return ((mz + o // 4) % 4) * 4 + (mx + o % 4) % 4

    barrier = pltpu.get_barrier_semaphore()

    def greet_req(o, carry):
        pl.semaphore_signal(barrier, inc=1, device_id={"req": req_peer(o)}, device_id_type=MESH)
        return carry

    def greet_kv(o, carry):
        peer = (kv + 2 * o) % n_kv
        pl.semaphore_signal(barrier, inc=1, device_id={"kv": peer}, device_id_type=MESH)
        return carry

    lax.fori_loop(1, n_req, greet_req, 0)
    lax.fori_loop(1, 4, greet_kv, 0)
    pl.semaphore_signal(
        barrier, inc=1, device_id={"kv": kv + 1 - 2 * (kv % 2)}, device_id_type=MESH
    )

    def remote(phase, o, axis, source, target):
        if axis == "req":
            name, peer = "req", req_peer(o)
        elif axis == "core":
            name, peer = "kv", kv + 1 - 2 * (kv % 2)
        else:
            name, peer = "kv", (kv + 2 * o) % n_kv
        if axis == "y":
            target = target.at[o]
        return pltpu.make_async_remote_copy(
            src_ref=source(peer), dst_ref=target, send_sem=send_sem.at[phase, o],
            recv_sem=recv_sem.at[phase, o], device_id={name: peer}, device_id_type=MESH,
        )

    def start_all(phase, count, axis, source, target):
        def body(o, carry):
            remote(phase, o, axis, source, target).start()
            return carry

        lax.fori_loop(1, count, body, 0)

    def wait_recv_all(phase, count, axis, source, target):
        def body(o, carry):
            remote(phase, o, axis, source, target).wait_recv()
            return carry

        lax.fori_loop(1, count, body, 0)

    def wait_send_all(phase, count, axis, source, target):
        def body(o, carry):
            remote(phase, o, axis, source, target).wait_send()
            return carry

        lax.fori_loop(1, count, body, 0)

    eye = iota((128, 128), 0) == iota((128, 128), 1)

    def column(row):
        return jnp.sum(jnp.where(eye, row, 0.0), 1, keepdims=True)

    def wide_row(ref):
        return jnp.concatenate([ref[i : i + 1, :] for i in range(ref.shape[0])], 1)

    slots = slots_ref[...]
    owner = (slots * 43691) >> 17
    page = slots - owner * PAGES
    home = owner >> 7
    place = page * 128 + (owner & 127)
    home_f = home.astype(F32)
    place_f = place.astype(F32)
    home_row = jnp.concatenate([home_f[i : i + 1] for i in range(3)], 1)
    place_row = jnp.concatenate([place_f[i : i + 1] for i in range(3)], 1)
    home_col = jnp.concatenate([column(home_f[i : i + 1]) for i in range(3)], 0)
    place_col = jnp.concatenate([column(place_f[i : i + 1]) for i in range(3)], 0)
    home_hot = (home_row == iota((16, blocks), 0).astype(F32)).astype(F32).astype(BF16)
    place_hot = (place_col == iota((blocks, blocks), 1).astype(F32)).astype(F32).astype(BF16)
    present = dot_nn(home_hot, place_hot)
    pm_send[...] = jnp.zeros_like(pm_send)
    for j in range(PAGES):
        pm_send[:, j, :] = present[:, 128 * j : 128 * (j + 1)]

    pl.semaphore_wait(barrier, n_req + 3)
    presence = (0, n_req, "req", lambda peer: pm_send.at[peer], pm_recv.at[me])
    start_all(*presence)
    pm_recv[pl.ds(me, 1)] = pm_send[pl.ds(me, 1)]

    order_row = home_row * 384.0 + place_row
    order_col = home_col * 384.0 + place_col
    before = (order_col < order_row).astype(F32)
    slot_row = jnp.sum(before, 0, keepdims=True) + 8.0 * home_row
    after = (order_row < order_col).astype(F32)
    slot_col = jnp.sum(after, 1, keepdims=True) + 8.0 * home_col
    n_slot = n_req * PAD

    len_row = lens_ref[pl.ds(me, 1), :].astype(F32)
    len_col = column(len_row)
    lane = iota((rows, 256), 1)
    frequency = jnp.exp((lane & 31).astype(F32) * (-9.210340371976184 / 32.0))
    angles = len_col * frequency
    cosines = jnp.cos(angles)
    sines = jnp.sin(angles)
    upper = (lane & 63) >= 32
    for load in loads[:4]:
        load.wait()
    values = hid[...].astype(F32)
    scale = lax.rsqrt(jnp.mean(values * values, -1, keepdims=True) + 1e-05)
    normed = (values * scale * wide_row(gain_ref)).astype(BF16)
    qk = dot_nt(normed, wqkv[pl.ds(0, 256), :])
    value_new[...] = dot_nt(normed, wqkv[pl.ds(256, 64), :]).astype(BF16)
    swapped = jnp.where(upper, pltpu.roll(qk, 32, 1), pltpu.roll(qk, 224, 1))
    turned = qk * cosines + jnp.where(upper, swapped, -swapped) * sines
    turned = jnp.where(lane < 192, turned * 0.125, turned).astype(BF16)
    rotated[...] = turned

    wait_recv_all(*presence)
    held = pm_recv[...].reshape(128, 128)
    held_b = held.astype(BF16)
    r0, c0 = iota((128, 128), 0), iota((128, 128), 1)
    ahead = (r0 < c0).astype(F32).astype(BF16)
    earlier = (((r0 >> 3) == (c0 >> 3)) & (c0 < r0)).astype(F32).astype(BF16)
    ones = jnp.ones((128, 128), BF16)
    counts = dot_nn(held_b, ahead) + dot_nn(dot_nn(earlier, held_b).astype(BF16), ones)
    source_slot = held * (counts + ((r0 >> 3) * PAD).astype(F32))
    page_slot = jnp.sum(source_slot.reshape(16, 8, 128), 0)
    page_row = jnp.concatenate([page_slot[j : j + 1] for j in range(PAGES)], 1)
    page_col = jnp.concatenate([column(page_slot[j : j + 1]) for j in range(PAGES)], 0)
    pick = (iota((n_slot, blocks), 0).astype(F32) == page_row).astype(F32).astype(BF16)
    gather_t[...] = (iota((blocks, n_slot), 1).astype(F32) == page_col).astype(F32).astype(BF16)
    extended = []
    for j in range(PAGES):
        used = jnp.clip(len_col - 128.0 * j, 0.0, 128.0)
        extended.append(jnp.where(lane < 192, turned.astype(F32), used).astype(BF16))
    q_send[...] = dot_nn(pick, jnp.concatenate(extended, 0)).astype(BF16)

    def slot_rows(index):
        return pl.ds(pl.multiple_of(index * PAD, PAD), PAD)

    queries = (1, n_req, "req", lambda peer: q_send.at[slot_rows(peer)], q_recv.at[slot_rows(me)])
    start_all(*queries)
    loads[6].wait()
    share_w = remote(0, 0, "core", lambda peer: wout, wout_peer)
    share_w.start()
    q_recv[slot_rows(me), :] = q_send[slot_rows(me), :]
    place_slot = (slot_col == iota((blocks, n_slot), 1).astype(F32)).astype(F32).astype(BF16)
    wait_recv_all(*queries)
    arrived = dot_nn(place_slot, q_recv[...])
    zeros = jnp.zeros((blocks, HD), BF16)
    for q in range(3):
        head = arrived[:, HD * q : HD * (q + 1)].astype(BF16)
        q6[q] = jnp.concatenate([head, zeros], 1)
        q6[q + 3] = jnp.concatenate([zeros, head], 1)
    limit = arrived[:, 192:256]
    thr[...] = jnp.concatenate([limit, limit], 1)

    loads[4].wait()
    loads[5].wait()
    wide_r, wide_c = iota((96, 256), 0), iota((96, 256), 1)
    position = jnp.where((wide_r & 15) == (wide_c & 15), 2 * (wide_c >> 4), 1 << 20).astype(F32)
    stat_lane = iota((16, HD), 1)

    def some_groups(step, carry):
        at = [pl.ds(pl.multiple_of((step * 4 + k) * 16, 16), 16) for k in range(4)]
        scores = []
        for here in at:
            query = q6[:, here, :].reshape(96, 128)
            bound = thr[here, :]
            bound = jnp.concatenate([bound] * 3 + [bound - 1.0] * 3, 0)
            bound = jnp.concatenate([bound, bound], 1)
            mine = []
            for c in range(4):
                keys = jnp.concatenate(
                    [kbuf[here, 128 * i : 128 * (i + 1)] for i in range(16 * c, 16 * c + 16)], 0
                )
                mine.append(jnp.where(position < bound - 32.0 * c, dot_nt(query, keys), LOW))
            scores.append(mine)
        tops, weights, totals = [], [], []
        for mine in scores:
            top = jnp.maximum(jnp.maximum(mine[0], mine[1]), jnp.maximum(mine[2], mine[3]))
            top = jnp.max(top, 1, keepdims=True)
            top = jnp.maximum(jnp.maximum(top[:48], top[48:]), -1e29)
            top_2 = jnp.concatenate([top, top], 0)
            these = [jnp.exp(s - top_2) for s in mine]
            total = jnp.sum((these[0] + these[1]) + (these[2] + these[3]), 1, keepdims=True)
            tops.append(top)
            weights.append([w.astype(BF16) for w in these])
            totals.append(total[:48] + total[48:])
        for here, top, these, total in zip(at, tops, weights, totals):
            numer = jnp.zeros((96, 128), F32)
            for c in range(4):
                vals = jnp.concatenate(
                    [vbuf[here, 128 * i : 128 * (i + 1)] for i in range(16 * c, 16 * c + 16)], 0
                )
                numer = numer + dot_nn(these[c], vals)
            numer = numer[:48, :HD] + numer[48:, HD:]
            some = total > 0.0
            safe = jnp.where(some, total, 1.0)
            numer = numer / safe
            lse = jnp.where(some, top + jnp.log(safe), LOW)
            pieces = [numer[16 * q : 16 * (q + 1)] for q in range(3)]
            stats = jnp.zeros((16, HD), F32)
            for q in range(3):
                for t, term in enumerate(split_3(lse[16 * q : 16 * (q + 1)])):
                    stats = jnp.where(stat_lane == 16 * t + q, term, stats)
            part[here, :] = jnp.concatenate(pieces + [stats], 1).astype(BF16)
        return carry

    lax.fori_loop(0, blocks // (16 * 4), some_groups, 0)

    slot_place = (iota((n_slot, blocks), 0).astype(F32) == slot_row).astype(F32).astype(BF16)
    part_send[...] = dot_nn(slot_place, part[...]).astype(BF16)
    partials = (
        2, n_req, "req", lambda peer: part_send.at[slot_rows(peer)], part_recv.at[slot_rows(me)],
    )
    start_all(*partials)
    part_recv[slot_rows(me), :] = part_send[slot_rows(me), :]
    own_q = rotated[...].astype(F32)
    own_k = own_q[:, 192:256]
    own_v = value_new[...].astype(F32)
    own_score = [
        jnp.sum(own_q[:, HD * q : HD * (q + 1)] * own_k, 1, keepdims=True) for q in range(3)
    ]
    wait_recv_all(*partials)
    pages = dot_nn(gather_t[...], part_recv[...])
    attended = []
    for q in range(3):
        lses, outs = [own_score[q]], [own_v]
        for j in range(PAGES):
            piece = pages[128 * j : 128 * (j + 1)]
            lses.append(
                piece[:, 192 + q : 193 + q]
                + piece[:, 208 + q : 209 + q]
                + piece[:, 224 + q : 225 + q]
            )
            outs.append(piece[:, HD * q : HD * (q + 1)])
        peak = jnp.maximum(jnp.maximum(lses[0], lses[1]), jnp.maximum(lses[2], lses[3]))
        shares = [jnp.exp(value - peak) for value in lses]
        whole = (shares[0] + shares[1]) + (shares[2] + shares[3])
        summed = shares[0] * outs[0] + shares[1] * outs[1]
        summed = summed + shares[2] * outs[2] + shares[3] * outs[3]
        attended.append((summed / whole).astype(BF16))
    attended = jnp.concatenate(attended, 1)

    core = kv % 2
    att[...] = jnp.concatenate([attended, jnp.zeros((rows, HD), BF16)], 1).reshape(4, 2, 16, 256)
    swap = remote(3, 0, "core", lambda peer: att.at[:, 1 - core], att_peer)
    swap.start()

    def token_rows(index):
        return pl.ds(pl.multiple_of(index * 16, 16), 16)

    own_rows = att[:, pl.ds(core, 1)].reshape(64, 256)[:, :192]
    share_w.wait_recv()
    swap.wait_recv()
    peer_rows = att_peer[...].reshape(64, 256)[:, :192]
    for n in range(0, model, 512):
        part_n = dot_nn(own_rows, wout[:, n : n + 512]) + dot_nn(peer_rows, wout_peer[:, n : n + 512])
        proj[:, :, n : n + 512] = part_n.astype(BF16).reshape(4, 16, 512)
    sums = (3, 4, "y", lambda peer: proj.at[peer // 2], proj_recv)
    start_all(*sums)
    expert_row = iota((128, 16), 0)
    chosen = jnp.zeros((128, 16), F32)
    for k in range(8):
        chosen = chosen + (routes_ref[k : k + 1, :] == expert_row).astype(F32)
    eye_16 = (iota((16, 16), 0) == iota((16, 16), 1)).astype(F32).astype(BF16)
    chosen = dot_nt(eye_16, chosen.astype(BF16))
    own_proj = proj[pl.ds(kv // 2, 1)].reshape(16, model).astype(F32)
    wait_recv_all(*sums)
    after_attn = hid[token_rows(kv), :].astype(F32)
    total = own_proj
    for k in range(1, 4):
        total = total + proj_recv[k].astype(F32)
    after_attn = after_attn + total
    scale = lax.rsqrt(jnp.mean(after_attn * after_attn, -1, keepdims=True) + 1e-05)
    moe_in = (after_attn * scale * wide_row(moe_gain_ref)).astype(BF16)
    logits = dot_nt(moe_in, router_ref[...])
    logits = jnp.concatenate([logits] * 4, 1)
    logits = jnp.where(chosen > 0.0, logits, LOW)
    gates = jnp.exp(logits - jnp.max(logits, 1, keepdims=True))
    gates = gates / jnp.sum(gates, 1, keepdims=True)
    high, middle, low = split_3(gates)
    tok_send[:, :model] = moe_in
    tok_send[:, model:] = jnp.concatenate(
        [high[:, :32], middle[:, :32], low[:, :32], jnp.zeros((16, 32), F32)], 1
    ).astype(BF16)

    def offset(s):
        k = s // 4
        return k + (k // 2) * (5 - 2 * k), s % 4

    def token_copy(s):
        oz, ox = offset(s)
        return pltpu.make_async_remote_copy(
            src_ref=tok_send, dst_ref=tok.at[token_rows(s)], send_sem=send_sem.at[4, s],
            recv_sem=recv_sem.at[4, s],
            device_id={"req": ((mz + oz) % 4) * 4 + (mx + ox) % 4}, device_id_type=MESH,
        )

    def back_copy(s):
        oz, ox = offset(s)
        return pltpu.make_async_remote_copy(
            src_ref=mixed_send.at[token_rows(s)], dst_ref=mixed_recv.at[s],
            send_sem=send_sem.at[5, s], recv_sem=recv_sem.at[5, s],
            device_id={"req": ((mz - oz + 4) % 4) * 4 + (mx - ox + 4) % 4}, device_id_type=MESH,
        )

    def each(first, last, action):
        def body(s, carry):
            action(s)
            return carry

        lax.fori_loop(first, last, body, 0)

    each(1, n_req, lambda s: token_copy(s).start())
    tok[0:16, :] = tok_send[...]
    loads[7].wait()
    loads[8].wait()
    gate_lane = iota((CHUNK, 128), 1)

    def chunk_step(k, carry):
        first, last = lax.max(k * (CHUNK // 16), 1), (k + 1) * (CHUNK // 16)
        each(first, last, lambda s: token_copy(s).wait_recv())
        here = pl.ds(pl.multiple_of(k * CHUNK, CHUNK), CHUNK)
        inputs = tok[here, :model]
        gate_all = tok[here, model:].astype(F32)
        outs = []
        for e in range(2):
            acts = []
            for f in range(0, FFE, 256):
                gate = dot_nn(inputs, up[e, :, f : f + 256])
                lift = dot_nn(inputs, up[e, :, FFE + f : FFE + f + 256])
                acts.append((gate * jax.nn.sigmoid(gate) * lift).astype(BF16))
            act = jnp.concatenate(acts, 1)
            mine = ((gate_lane & 31) == 2 * me + e) & (gate_lane < 96)
            weight = jnp.sum(jnp.where(mine, gate_all, 0.0), 1, keepdims=True)
            for n in range(0, model, 256):
                made = dot_nn(act, down[e, :, n : n + 256]).astype(BF16).astype(F32) * weight
                if e == 0:
                    mixed[:, n : n + 256] = made
                else:
                    made = mixed[:, n : n + 256] + made
                    mixed_send[here, n : n + 256] = made.astype(BF16)
        each(first, last, lambda s: back_copy(s).start())
        return carry

    lax.fori_loop(0, 256 // CHUNK, chunk_step, 0)
    result = mixed_send[0:16, :].astype(F32)
    each(1, n_req, lambda s: back_copy(s).wait_recv())
    for d in range(1, n_req):
        result = result + mixed_recv[d].astype(F32)
    out_ref[...] = (after_attn + result).astype(BF16)
    each(1, n_req, lambda s: token_copy(s).wait_send())
    each(1, n_req, lambda s: back_copy(s).wait_send())
    share_w.wait_send()
    swap.wait_send()
    for exchange in (presence, queries, partials, sums):
        wait_send_all(*exchange)


def shards(
    hidden_in, attn_gain, w_query, w_key, w_value, w_out, k_cache, v_cache, cache_len, block_slot,
    moe_gain, w_router, w_gate_up, w_down, routes,
):
    any_spec = pl.BlockSpec(memory_space=pl.ANY)
    vmem = pl.BlockSpec(memory_space=pltpu.VMEM)
    blocks = k_cache.shape[0]
    model = hidden_in.shape[1]
    rows = hidden_in.shape[0]
    n_slot = 16 * PAD
    scratch = [
        ((rows, model), BF16), ((320, model), BF16), ((192, model), BF16),
        ((blocks, 8192), BF16), ((blocks, 8192), BF16),
        (w_gate_up.shape, BF16), (w_down.shape, BF16),
        ((16, 8, 128), F32), ((16, 8, 128), F32),
        ((n_slot, 256), BF16), ((n_slot, 256), BF16),
        ((6, blocks, 128), BF16), ((blocks, 128), F32),
        ((blocks, 256), BF16), ((n_slot, 256), BF16), ((n_slot, 256), BF16),
        ((blocks, n_slot), BF16),
        ((rows, 256), BF16), ((rows, HD), BF16), ((4, 16, model), BF16), ((4, 16, model), BF16),
        ((4, 2, 16, 256), BF16), ((4, 16, 256), BF16), ((192, model), BF16),
        ((16, model + 128), BF16), ((256, model + 128), BF16),
        ((CHUNK, model), F32), ((256, model), BF16), ((16, 16, model), BF16),
    ]
    return pl.pallas_call(
        kernel,
        out_shape=jax.ShapeDtypeStruct((16, model), BF16),
        in_specs=[
            any_spec, vmem, any_spec, any_spec, any_spec, any_spec, any_spec, any_spec, vmem, vmem,
            vmem, vmem, any_spec, any_spec, vmem,
        ],
        out_specs=vmem,
        scratch_shapes=[pltpu.VMEM(shape, dtype) for shape, dtype in scratch]
        + [
            pltpu.SemaphoreType.DMA((9,)),
            pltpu.SemaphoreType.DMA((6, 16)),
            pltpu.SemaphoreType.DMA((6, 16)),
        ],
        compiler_params=pltpu.CompilerParams(
            collective_id=0, has_side_effects=True, vmem_limit_bytes=56 << 20
        ),
    )(
        hidden_in, attn_gain.reshape(model // 128, 128), w_query, w_key, w_value, w_out,
        k_cache.reshape(blocks, 8192), v_cache.reshape(blocks, 8192),
        cache_len.reshape(16, 128), block_slot.reshape(3, 128),
        moe_gain.reshape(model // 128, 128), w_router.T, w_gate_up, w_down, routes.T,
    )


def solution(mesh):
    placed = (
        P("req", None),
        P(),
        P("kv", None),
        P("kv", None),
        P("kv", None),
        P("kv", None),
        P("req", "kv", None),
        P("req", "kv", None),
        P(),
        P("req"),
        P(),
        P(),
        P("req", None, None),
        P("req", None, None),
        P(("req", "kv"), None),
    )
    return jax.shard_map(
        shards, mesh=mesh, in_specs=placed, out_specs=P(("req", "kv"), None), check_vma=False
    )
```

```python
import jax
import jax.numpy as jnp
from jax import lax
from jax.experimental import pallas as pl
from jax.experimental.pallas import tpu as pltpu
from jax.sharding import PartitionSpec as P

HD = 64
FFE = 512
BLK = 128
PAGES = 3
PAD = 32
CHUNK = 64
ORDER = [
    (0, 0), (0, 1), (3, 0), (0, 3), (1, 0), (0, 2), (2, 0), (1, 1),
    (3, 3), (1, 3), (3, 1), (2, 1), (1, 2), (2, 3), (3, 2), (2, 2),
]
LOW = -1e30
MESH = pl.DeviceIdType.MESH
F32 = jnp.float32
BF16 = jnp.bfloat16


def dot_nt(left, right):
    return lax.dot_general(left, right, (((1,), (1,)), ((), ())), preferred_element_type=F32)


def dot_nn(left, right):
    return jnp.dot(left, right, preferred_element_type=F32)


def iota(shape, axis):
    return lax.broadcasted_iota(jnp.int32, shape, axis)


def split_3(value):
    high = value.astype(BF16).astype(F32)
    rest = value - high
    middle = rest.astype(BF16).astype(F32)
    return high, middle, rest - middle


def kernel(
    hidden_hbm, gain_ref, wq_hbm, wk_hbm, wv_hbm, wout_hbm, k_hbm, v_hbm, lens_ref, slots_ref,
    moe_gain_ref, router_ref, up_hbm, down_hbm, routes_ref,
    out_ref,
    hid, wqkv, wout, kbuf, vbuf, up, down,
    pm_send, pm_recv, q_send, q_recv, q6, thr, part, part_send, part_recv, gather_t,
    rotated, value_new, proj, proj_recv, att, att_peer, wout_peer,
    mask_send, mask_recv, slot_place, tok_send, tok, mixed, mixed_send, mixed_recv,
    local_sem, send_sem, recv_sem,
):
    me = lax.axis_index("req")
    kv = lax.axis_index("kv")
    mz, mx = me // 4, me % 4
    n_req, n_kv = 16, 8
    rows, model = hid.shape
    blocks = kbuf.shape[0]

    loads = [
        (hidden_hbm, hid), (wq_hbm, wqkv.at[pl.ds(0, 192)]), (wk_hbm, wqkv.at[pl.ds(192, 64)]),
        (wv_hbm, wqkv.at[pl.ds(256, 64)]), (k_hbm, kbuf), (v_hbm, vbuf), (wout_hbm, wout),
        (up_hbm, up), (down_hbm, down),
    ]
    loads = [
        pltpu.make_async_copy(src, dst, local_sem.at[i]) for i, (src, dst) in enumerate(loads)
    ]
    for load in loads:
        load.start()

    def req_peer(o):
        return ((mz + o // 4) % 4) * 4 + (mx + o % 4) % 4

    barrier = pltpu.get_barrier_semaphore()

    def greet_req(o, carry):
        pl.semaphore_signal(barrier, inc=1, device_id={"req": req_peer(o)}, device_id_type=MESH)
        return carry

    def greet_kv(o, carry):
        peer = (kv + 2 * o) % n_kv
        pl.semaphore_signal(barrier, inc=1, device_id={"kv": peer}, device_id_type=MESH)
        return carry

    lax.fori_loop(1, n_req, greet_req, 0)
    lax.fori_loop(1, 4, greet_kv, 0)
    pl.semaphore_signal(
        barrier, inc=1, device_id={"kv": kv + 1 - 2 * (kv % 2)}, device_id_type=MESH
    )

    def remote(phase, o, axis, source, target):
        if axis == "req":
            name, peer = "req", req_peer(o)
        elif axis == "core":
            name, peer = "kv", kv + 1 - 2 * (kv % 2)
        else:
            name, peer = "kv", (kv + 2 * o) % n_kv
        if axis == "y":
            target = target.at[o]
        return pltpu.make_async_remote_copy(
            src_ref=source(peer), dst_ref=target, send_sem=send_sem.at[phase, o],
            recv_sem=recv_sem.at[phase, o], device_id={name: peer}, device_id_type=MESH,
        )

    def far_req(s):
        oz, ox = ORDER[s]
        return ((mz + oz) % 4) * 4 + (mx + ox) % 4

    def near_req(s):
        oz, ox = ORDER[s]
        return ((mz + 4 - oz) % 4) * 4 + (mx + 4 - ox) % 4

    def token_rows(index):
        return pl.ds(pl.multiple_of(index * 16, 16), 16)

    def slot_copy(phase, s, source, target, peer):
        return pltpu.make_async_remote_copy(
            src_ref=source, dst_ref=target, send_sem=send_sem.at[phase, s],
            recv_sem=recv_sem.at[phase, s], device_id={"req": peer}, device_id_type=MESH,
        )

    def mask_copy(s):
        return slot_copy(6, s, mask_send, mask_recv.at[pl.ds(16 * s, 16)], far_req(s))

    def token_copy(s):
        return slot_copy(4, s, tok_send, tok.at[pl.ds(16 * s, 16)], far_req(s))

    def back_copy(s):
        return slot_copy(5, s, mixed_send.at[pl.ds(16 * s, 16)], mixed_recv.at[s], near_req(s))

    def each(first, last, action):
        for s in range(first, last):
            action(s)

    def start_all(phase, count, axis, source, target):
        def body(o, carry):
            remote(phase, o, axis, source, target).start()
            return carry

        lax.fori_loop(1, count, body, 0)

    def wait_recv_all(phase, count, axis, source, target):
        def body(o, carry):
            remote(phase, o, axis, source, target).wait_recv()
            return carry

        lax.fori_loop(1, count, body, 0)

    def wait_send_all(phase, count, axis, source, target):
        def body(o, carry):
            remote(phase, o, axis, source, target).wait_send()
            return carry

        lax.fori_loop(1, count, body, 0)

    eye = iota((128, 128), 0) == iota((128, 128), 1)

    def column(row):
        return jnp.sum(jnp.where(eye, row, 0.0), 1, keepdims=True)

    def wide_row(ref):
        return jnp.concatenate([ref[i : i + 1, :] for i in range(ref.shape[0])], 1)

    slots = slots_ref[...]
    owner = (slots * 43691) >> 17
    page = slots - owner * PAGES
    home = owner >> 7
    place = page * 128 + (owner & 127)
    home_f = home.astype(F32)
    place_f = place.astype(F32)
    home_row = jnp.concatenate([home_f[i : i + 1] for i in range(3)], 1)
    place_row = jnp.concatenate([place_f[i : i + 1] for i in range(3)], 1)
    home_col = jnp.concatenate([column(home_f[i : i + 1]) for i in range(3)], 0)
    place_col = jnp.concatenate([column(place_f[i : i + 1]) for i in range(3)], 0)
    home_hot = (home_row == iota((16, blocks), 0).astype(F32)).astype(F32).astype(BF16)
    place_hot = (place_col == iota((blocks, blocks), 1).astype(F32)).astype(F32).astype(BF16)
    present = dot_nn(home_hot, place_hot)
    pm_send[...] = jnp.zeros_like(pm_send)
    for j in range(PAGES):
        pm_send[:, j, :] = present[:, 128 * j : 128 * (j + 1)]

    pl.semaphore_wait(barrier, n_req + 3)
    presence = (0, n_req, "req", lambda peer: pm_send.at[peer], pm_recv.at[me])
    start_all(*presence)
    pm_recv[pl.ds(me, 1)] = pm_send[pl.ds(me, 1)]

    order_row = home_row * 384.0 + place_row
    order_col = home_col * 384.0 + place_col
    before = (order_col < order_row).astype(F32)
    slot_row = jnp.sum(before, 0, keepdims=True) + 8.0 * home_row
    after = (order_row < order_col).astype(F32)
    slot_col = jnp.sum(after, 1, keepdims=True) + 8.0 * home_col
    n_slot = n_req * PAD

    len_row = lens_ref[pl.ds(me, 1), :].astype(F32)
    len_col = column(len_row)
    lane = iota((rows, 256), 1)
    frequency = jnp.exp((lane & 31).astype(F32) * (-9.210340371976184 / 32.0))
    angles = len_col * frequency
    cosines = jnp.cos(angles)
    sines = jnp.sin(angles)
    upper = (lane & 63) >= 32
    for load in loads[:4]:
        load.wait()
    values = hid[...].astype(F32)
    scale = lax.rsqrt(jnp.mean(values * values, -1, keepdims=True) + 1e-05)
    normed = (values * scale * wide_row(gain_ref)).astype(BF16)
    qk = dot_nt(normed, wqkv[pl.ds(0, 256), :])
    value_new[...] = dot_nt(normed, wqkv[pl.ds(256, 64), :]).astype(BF16)
    swapped = jnp.where(upper, pltpu.roll(qk, 32, 1), pltpu.roll(qk, 224, 1))
    turned = qk * cosines + jnp.where(upper, swapped, -swapped) * sines
    turned = jnp.where(lane < 192, turned * 0.125, turned).astype(BF16)
    rotated[...] = turned

    wait_recv_all(*presence)
    held = pm_recv[...].reshape(128, 128)
    held_b = held.astype(BF16)
    r0, c0 = iota((128, 128), 0), iota((128, 128), 1)
    ahead = (r0 < c0).astype(F32).astype(BF16)
    earlier = (((r0 >> 3) == (c0 >> 3)) & (c0 < r0)).astype(F32).astype(BF16)
    ones = jnp.ones((128, 128), BF16)
    counts = dot_nn(held_b, ahead) + dot_nn(dot_nn(earlier, held_b).astype(BF16), ones)
    source_slot = held * (counts + ((r0 >> 3) * PAD).astype(F32))
    page_slot = jnp.sum(source_slot.reshape(16, 8, 128), 0)
    page_row = jnp.concatenate([page_slot[j : j + 1] for j in range(PAGES)], 1)
    page_col = jnp.concatenate([column(page_slot[j : j + 1]) for j in range(PAGES)], 0)
    pick = (iota((n_slot, blocks), 0).astype(F32) == page_row).astype(F32).astype(BF16)
    gather_t[...] = (iota((blocks, n_slot), 1).astype(F32) == page_col).astype(F32).astype(BF16)
    extended = []
    for j in range(PAGES):
        used = jnp.clip(len_col - 128.0 * j, 0.0, 128.0)
        extended.append(jnp.where(lane < 192, turned.astype(F32), used).astype(BF16))
    q_send[...] = dot_nn(pick, jnp.concatenate(extended, 0)).astype(BF16)

    def slot_rows(index):
        return pl.ds(pl.multiple_of(index * PAD, PAD), PAD)

    queries = (1, n_req, "req", lambda peer: q_send.at[slot_rows(peer)], q_recv.at[slot_rows(me)])
    start_all(*queries)
    expert_row = iota((128, 16), 0)
    chosen = jnp.zeros((128, 16), F32)
    for k in range(8):
        chosen = chosen + (routes_ref[k : k + 1, :] == expert_row).astype(F32)
    eye_16 = (iota((16, 16), 0) == iota((16, 16), 1)).astype(F32).astype(BF16)
    mask_send[...] = dot_nt(eye_16, chosen.astype(BF16)).astype(BF16)
    mask_recv[0:16, :] = mask_send[...]
    each(1, n_req, lambda s: mask_copy(s).start())
    loads[6].wait()
    share_w = remote(0, 0, "core", lambda peer: wout, wout_peer)
    share_w.start()
    q_recv[slot_rows(me), :] = q_send[slot_rows(me), :]
    place_slot = (slot_col == iota((blocks, n_slot), 1).astype(F32)).astype(F32).astype(BF16)
    slot_place[...] = (iota((n_slot, blocks), 0).astype(F32) == slot_row).astype(F32).astype(BF16)
    wait_recv_all(*queries)
    arrived = dot_nn(place_slot, q_recv[...])
    zeros = jnp.zeros((blocks, HD), BF16)
    for q in range(3):
        head = arrived[:, HD * q : HD * (q + 1)].astype(BF16)
        q6[q] = jnp.concatenate([head, zeros], 1)
        q6[q + 3] = jnp.concatenate([zeros, head], 1)
    limit = arrived[:, 192:256]
    thr[...] = jnp.concatenate([limit, limit], 1)

    loads[4].wait()
    loads[5].wait()
    wide_r, wide_c = iota((96, 256), 0), iota((96, 256), 1)
    position = jnp.where((wide_r & 15) == (wide_c & 15), 2 * (wide_c >> 4), 1 << 20).astype(F32)
    stat_lane = iota((16, HD), 1)

    def some_groups(step, carry):
        at = [pl.ds(pl.multiple_of((step * 8 + k) * 16, 16), 16) for k in range(8)]
        scores = []
        for here in at:
            query = q6[:, here, :].reshape(96, 128)
            bound = thr[here, :]
            bound = jnp.concatenate([bound] * 3 + [bound - 1.0] * 3, 0)
            bound = jnp.concatenate([bound, bound], 1)
            mine = []
            for c in range(4):
                keys = jnp.concatenate(
                    [kbuf[here, 128 * i : 128 * (i + 1)] for i in range(16 * c, 16 * c + 16)], 0
                )
                mine.append(jnp.where(position < bound - 32.0 * c, dot_nt(query, keys), LOW))
            scores.append(mine)
        tops, weights, totals = [], [], []
        for mine in scores:
            top = jnp.maximum(jnp.maximum(mine[0], mine[1]), jnp.maximum(mine[2], mine[3]))
            top = jnp.max(top, 1, keepdims=True)
            top = jnp.maximum(jnp.maximum(top[:48], top[48:]), -1e29)
            top_2 = jnp.concatenate([top, top], 0)
            these = [jnp.exp(s - top_2) for s in mine]
            total = jnp.sum((these[0] + these[1]) + (these[2] + these[3]), 1, keepdims=True)
            tops.append(top)
            weights.append([w.astype(BF16) for w in these])
            totals.append(total[:48] + total[48:])
        for here, top, these, total in zip(at, tops, weights, totals):
            numer = jnp.zeros((96, 128), F32)
            for c in range(4):
                vals = jnp.concatenate(
                    [vbuf[here, 128 * i : 128 * (i + 1)] for i in range(16 * c, 16 * c + 16)], 0
                )
                numer = numer + dot_nn(these[c], vals)
            numer = numer[:48, :HD] + numer[48:, HD:]
            some = total > 0.0
            safe = jnp.where(some, total, 1.0)
            numer = numer / safe
            lse = jnp.where(some, top + jnp.log(safe), LOW)
            pieces = [numer[16 * q : 16 * (q + 1)] for q in range(3)]
            stats = jnp.zeros((16, HD), F32)
            for q in range(3):
                for t, term in enumerate(split_3(lse[16 * q : 16 * (q + 1)])):
                    stats = jnp.where(stat_lane == 16 * t + q, term, stats)
            part[here, :] = jnp.concatenate(pieces + [stats], 1).astype(BF16)
        return carry

    lax.fori_loop(0, blocks // (16 * 8), some_groups, 0)

    part_send[...] = dot_nn(slot_place[...], part[...]).astype(BF16)
    partials = (
        2, n_req, "req", lambda peer: part_send.at[slot_rows(peer)], part_recv.at[slot_rows(me)],
    )
    start_all(*partials)
    part_recv[slot_rows(me), :] = part_send[slot_rows(me), :]
    own_q = rotated[...].astype(F32)
    own_k = own_q[:, 192:256]
    own_v = value_new[...].astype(F32)
    own_score = [
        jnp.sum(own_q[:, HD * q : HD * (q + 1)] * own_k, 1, keepdims=True) for q in range(3)
    ]
    wait_recv_all(*partials)
    pages = dot_nn(gather_t[...], part_recv[...])
    attended = []
    for q in range(3):
        lses, outs = [own_score[q]], [own_v]
        for j in range(PAGES):
            piece = pages[128 * j : 128 * (j + 1)]
            lses.append(
                piece[:, 192 + q : 193 + q]
                + piece[:, 208 + q : 209 + q]
                + piece[:, 224 + q : 225 + q]
            )
            outs.append(piece[:, HD * q : HD * (q + 1)])
        peak = jnp.maximum(jnp.maximum(lses[0], lses[1]), jnp.maximum(lses[2], lses[3]))
        shares = [jnp.exp(value - peak) for value in lses]
        whole = (shares[0] + shares[1]) + (shares[2] + shares[3])
        summed = shares[0] * outs[0] + shares[1] * outs[1]
        summed = summed + shares[2] * outs[2] + shares[3] * outs[3]
        attended.append((summed / whole).astype(BF16))
    attended = jnp.concatenate(attended, 1)

    core = kv % 2
    att[...] = jnp.concatenate([attended, jnp.zeros((rows, HD), BF16)], 1).reshape(4, 2, 16, 256)
    swap = remote(3, 0, "core", lambda peer: att.at[:, 1 - core], att_peer)
    swap.start()

    own_rows = att[:, pl.ds(core, 1)].reshape(64, 256)[:, :192]
    own_part = [dot_nn(own_rows, wout[:, n : n + 512]) for n in range(0, model, 512)]
    share_w.wait_recv()
    swap.wait_recv()
    peer_rows = att_peer[...].reshape(64, 256)[:, :192]
    for n in range(0, model, 512):
        part_n = own_part[n // 512] + dot_nn(peer_rows, wout_peer[:, n : n + 512])
        proj[:, :, n : n + 512] = part_n.astype(BF16).reshape(4, 16, 512)
    sums = (3, 4, "y", lambda peer: proj.at[peer // 2], proj_recv)
    start_all(*sums)
    own_proj = proj[pl.ds(kv // 2, 1)].reshape(16, model).astype(F32)
    wait_recv_all(*sums)
    after_attn = hid[token_rows(kv), :].astype(F32)
    total = own_proj
    for k in range(1, 4):
        total = total + proj_recv[k].astype(F32)
    after_attn = after_attn + total
    scale = lax.rsqrt(jnp.mean(after_attn * after_attn, -1, keepdims=True) + 1e-05)
    moe_in = (after_attn * scale * wide_row(moe_gain_ref)).astype(BF16)
    tok_send[...] = moe_in
    each(1, n_req, lambda s: token_copy(s).start())
    tok[0:16, :] = tok_send[...]
    loads[7].wait()
    loads[8].wait()
    gate_lane = iota((CHUNK, 128), 1)
    each(1, n_req, lambda s: mask_copy(s).wait_recv())
    for k in range(256 // CHUNK):
        first, last = max(k * (CHUNK // 16), 1), (k + 1) * (CHUNK // 16)
        each(first, last, lambda s: token_copy(s).wait_recv())
        here = pl.ds(k * CHUNK, CHUNK)
        inputs = tok[here, :]
        logits = jnp.concatenate([dot_nt(inputs, router_ref[...])] * 4, 1)
        logits = jnp.where(mask_recv[here, :].astype(F32) > 0.0, logits, LOW)
        gates = jnp.exp(logits - jnp.max(logits, 1, keepdims=True))
        gates = gates / jnp.sum(gates, 1, keepdims=True)
        for e in range(2):
            weight = jnp.sum(jnp.where(gate_lane == 2 * me + e, gates, 0.0), 1, keepdims=True)
            acts = []
            for f in range(0, FFE, 256):
                gate = dot_nn(inputs, up[e, :, f : f + 256])
                lift = dot_nn(inputs, up[e, :, FFE + f : FFE + f + 256])
                acts.append((gate * jax.nn.sigmoid(gate) * lift).astype(BF16))
            act = jnp.concatenate(acts, 1)
            for n in range(0, model, 256):
                made = dot_nn(act, down[e, :, n : n + 256]).astype(BF16).astype(F32) * weight
                if e == 0:
                    mixed[:, n : n + 256] = made
                else:
                    made = mixed[:, n : n + 256] + made
                    mixed_send[here, n : n + 256] = made.astype(BF16)
        each(first, last, lambda s: back_copy(s).start())

    result = mixed_send[0:16, :].astype(F32)
    for d in range(1, n_req):
        back_copy(d).wait_recv()
        result = result + mixed_recv[d].astype(F32)
    out_ref[...] = (after_attn + result).astype(BF16)
    each(1, n_req, lambda s: mask_copy(s).wait_send())
    each(1, n_req, lambda s: token_copy(s).wait_send())
    each(1, n_req, lambda s: back_copy(s).wait_send())
    share_w.wait_send()
    swap.wait_send()
    for exchange in (presence, queries, partials, sums):
        wait_send_all(*exchange)


def shards(
    hidden_in, attn_gain, w_query, w_key, w_value, w_out, k_cache, v_cache, cache_len, block_slot,
    moe_gain, w_router, w_gate_up, w_down, routes,
):
    any_spec = pl.BlockSpec(memory_space=pl.ANY)
    vmem = pl.BlockSpec(memory_space=pltpu.VMEM)
    blocks = k_cache.shape[0]
    model = hidden_in.shape[1]
    rows = hidden_in.shape[0]
    n_slot = 16 * PAD
    scratch = [
        ((rows, model), BF16), ((320, model), BF16), ((192, model), BF16),
        ((blocks, 8192), BF16), ((blocks, 8192), BF16),
        (w_gate_up.shape, BF16), (w_down.shape, BF16),
        ((16, 8, 128), F32), ((16, 8, 128), F32),
        ((n_slot, 256), BF16), ((n_slot, 256), BF16),
        ((6, blocks, 128), BF16), ((blocks, 128), F32),
        ((blocks, 256), BF16), ((n_slot, 256), BF16), ((n_slot, 256), BF16),
        ((blocks, n_slot), BF16),
        ((rows, 256), BF16), ((rows, HD), BF16), ((4, 16, model), BF16), ((4, 16, model), BF16),
        ((4, 2, 16, 256), BF16), ((4, 16, 256), BF16), ((192, model), BF16),
        ((16, 128), BF16), ((256, 128), BF16), ((n_slot, blocks), BF16),
        ((16, model), BF16), ((256, model), BF16),
        ((CHUNK, model), F32), ((256, model), BF16), ((16, 16, model), BF16),
    ]
    return pl.pallas_call(
        kernel,
        out_shape=jax.ShapeDtypeStruct((16, model), BF16),
        in_specs=[
            any_spec, vmem, any_spec, any_spec, any_spec, any_spec, any_spec, any_spec, vmem, vmem,
            vmem, vmem, any_spec, any_spec, vmem,
        ],
        out_specs=vmem,
        scratch_shapes=[pltpu.VMEM(shape, dtype) for shape, dtype in scratch]
        + [
            pltpu.SemaphoreType.DMA((9,)),
            pltpu.SemaphoreType.DMA((7, 16)),
            pltpu.SemaphoreType.DMA((7, 16)),
        ],
        compiler_params=pltpu.CompilerParams(
            collective_id=0, has_side_effects=True, vmem_limit_bytes=56 << 20
        ),
    )(
        hidden_in, attn_gain.reshape(model // 128, 128), w_query, w_key, w_value, w_out,
        k_cache.reshape(blocks, 8192), v_cache.reshape(blocks, 8192),
        cache_len.reshape(16, 128), block_slot.reshape(3, 128),
        moe_gain.reshape(model // 128, 128), w_router.T, w_gate_up, w_down, routes.T,
    )


def solution(mesh):
    placed = (
        P("req", None),
        P(),
        P("kv", None),
        P("kv", None),
        P("kv", None),
        P("kv", None),
        P("req", "kv", None),
        P("req", "kv", None),
        P(),
        P("req"),
        P(),
        P(),
        P("req", None, None),
        P("req", None, None),
        P(("req", "kv"), None),
    )
    return jax.shard_map(
        shards, mesh=mesh, in_specs=placed, out_specs=P(("req", "kv"), None), check_vma=False
    )
```

```python
import jax
import jax.numpy as jnp
from jax import lax
from jax.experimental import pallas as pl
from jax.experimental.pallas import tpu as pltpu
from jax.sharding import PartitionSpec as P

HD = 64
FFE = 512
BLK = 128
PAGES = 3
PAD = 32
ORDER = [
    (0, 0), (0, 1), (0, 3), (1, 0), (3, 0), (0, 2), (2, 0), (1, 1),
    (3, 3), (1, 3), (3, 1), (1, 2), (3, 2), (2, 1), (2, 3), (2, 2),
]
FAR = [oz * 4 + ox for oz, ox in reversed(ORDER) if (oz, ox) != (0, 0)]
CHUNKS = [(0, 4), (4, 7), (7, 11), (11, 16)]
X_FIRST = [(1, 1), (3, 3), (1, 2), (3, 2)]
LOW = -1e30
MESH = pl.DeviceIdType.MESH
F32 = jnp.float32
BF16 = jnp.bfloat16


def dot_nt(left, right):
    return lax.dot_general(left, right, (((1,), (1,)), ((), ())), preferred_element_type=F32)


def dot_nn(left, right):
    return jnp.dot(left, right, preferred_element_type=F32)


def iota(shape, axis):
    return lax.broadcasted_iota(jnp.int32, shape, axis)


def split_3(value):
    high = value.astype(BF16).astype(F32)
    rest = value - high
    middle = rest.astype(BF16).astype(F32)
    return high, middle, rest - middle


def kernel(
    hidden_hbm, gain_ref, wq_hbm, wk_hbm, wv_hbm, wout_hbm, k_hbm, v_hbm, lens_ref, slots_ref,
    moe_gain_ref, router_ref, up_hbm, down_hbm, routes_ref,
    out_ref,
    hid, wqkv, wout, kbuf, vbuf, up, down,
    pm_send, pm_recv, q_send, q_recv, q6, thr, part, part_send, part_recv, gather_t,
    rotated, value_new, proj, proj_recv, att, att_peer, wout_peer,
    mask_send, mask_recv, slot_place, tok_send, tok, mixed, mixed_send, mixed_recv,
    local_sem, send_sem, recv_sem,
):
    me = lax.axis_index("req")
    kv = lax.axis_index("kv")
    mz, mx = me // 4, me % 4
    n_req, n_kv = 16, 8
    rows, model = hid.shape
    blocks = kbuf.shape[0]

    loads = [
        (hidden_hbm, hid), (wq_hbm, wqkv.at[pl.ds(0, 192)]), (wk_hbm, wqkv.at[pl.ds(192, 64)]),
        (wv_hbm, wqkv.at[pl.ds(256, 64)]), (k_hbm, kbuf), (v_hbm, vbuf), (wout_hbm, wout),
        (up_hbm, up), (down_hbm, down),
    ]
    loads = [
        pltpu.make_async_copy(src, dst, local_sem.at[i]) for i, (src, dst) in enumerate(loads)
    ]
    for load in loads:
        load.start()

    def req_peer(o):
        return ((mz + o // 4) % 4) * 4 + (mx + o % 4) % 4

    barrier = pltpu.get_barrier_semaphore()

    for o in FAR:
        pl.semaphore_signal(barrier, inc=1, device_id={"req": req_peer(o)}, device_id_type=MESH)

    def greet_kv(o, carry):
        peer = (kv + 2 * o) % n_kv
        pl.semaphore_signal(barrier, inc=1, device_id={"kv": peer}, device_id_type=MESH)
        return carry

    lax.fori_loop(1, 4, greet_kv, 0)
    pl.semaphore_signal(
        barrier, inc=1, device_id={"kv": kv + 1 - 2 * (kv % 2)}, device_id_type=MESH
    )

    def remote(phase, o, axis, source, target):
        if axis == "req":
            name, peer = "req", req_peer(o)
        elif axis == "core":
            name, peer = "kv", kv + 1 - 2 * (kv % 2)
        else:
            name, peer = "kv", (kv + 2 * o) % n_kv
        if axis == "y":
            target = target.at[o]
        return pltpu.make_async_remote_copy(
            src_ref=source(peer), dst_ref=target, send_sem=send_sem.at[phase, o],
            recv_sem=recv_sem.at[phase, o], device_id={name: peer}, device_id_type=MESH,
        )

    def far_req(s):
        oz, ox = ORDER[s]
        return ((mz + oz) % 4) * 4 + (mx + ox) % 4

    def near_req(s):
        oz, ox = ORDER[s]
        return ((mz + 4 - oz) % 4) * 4 + (mx + 4 - ox) % 4

    def token_rows(index):
        return pl.ds(pl.multiple_of(index * 16, 16), 16)

    def slot_copy(phase, s, source, target, peer):
        return pltpu.make_async_remote_copy(
            src_ref=source, dst_ref=target, send_sem=send_sem.at[phase, s],
            recv_sem=recv_sem.at[phase, s], device_id={"req": peer}, device_id_type=MESH,
        )

    def mask_copy(s):
        return slot_copy(6, s, mask_send, mask_recv.at[pl.ds(16 * s, 16)], far_req(s))

    core = kv % 2

    def token_copy(s):
        oz, ox = ORDER[s]
        if s < 7:
            source, peer = tok_send, far_req(s)
        else:
            by_x, by_z = ORDER.index((0, ox)), ORDER.index((oz, 0))
            to_z = ((mz + oz) % 4) * 4 + mx
            to_x = mz * 4 + (mx + ox) % 4
            if (oz, ox) == (2, 2):
                source = tok.at[token_rows(by_x + core * (by_z - by_x))]
                peer = to_z + core * (to_x - to_z)
            elif (oz, ox) in X_FIRST:
                source, peer = tok.at[token_rows(by_x)], to_z
            else:
                source, peer = tok.at[token_rows(by_z)], to_x
        return slot_copy(4, s, source, tok.at[token_rows(s)], peer)

    def back_copy(s):
        return slot_copy(5, s, mixed_send.at[pl.ds(16 * s, 16)], mixed_recv.at[s], near_req(s))

    def each(first, last, action):
        for s in range(first, last):
            action(s)

    def start_all(phase, count, axis, source, target):
        def body(o, carry):
            remote(phase, o, axis, source, target).start()
            return carry

        lax.fori_loop(1, count, body, 0)

    def wait_recv_all(phase, count, axis, source, target):
        def body(o, carry):
            remote(phase, o, axis, source, target).wait_recv()
            return carry

        lax.fori_loop(1, count, body, 0)

    def wait_send_all(phase, count, axis, source, target):
        def body(o, carry):
            remote(phase, o, axis, source, target).wait_send()
            return carry

        lax.fori_loop(1, count, body, 0)

    eye = iota((128, 128), 0) == iota((128, 128), 1)

    def column(row):
        return jnp.sum(jnp.where(eye, row, 0.0), 1, keepdims=True)

    def wide_row(ref):
        return jnp.concatenate([ref[i : i + 1, :] for i in range(ref.shape[0])], 1)

    slots = slots_ref[...]
    owner = (slots * 43691) >> 17
    page = slots - owner * PAGES
    home = owner >> 7
    place = page * 128 + (owner & 127)
    home_f = home.astype(F32)
    place_f = place.astype(F32)
    home_row = jnp.concatenate([home_f[i : i + 1] for i in range(3)], 1)
    place_row = jnp.concatenate([place_f[i : i + 1] for i in range(3)], 1)
    home_col = jnp.concatenate([column(home_f[i : i + 1]) for i in range(3)], 0)
    place_col = jnp.concatenate([column(place_f[i : i + 1]) for i in range(3)], 0)
    home_hot = (home_row == iota((16, blocks), 0).astype(F32)).astype(F32).astype(BF16)
    order_row = home_row * 384.0 + place_row
    order_col = home_col * 384.0 + place_col
    before = (order_col < order_row).astype(F32)
    slot_row = jnp.sum(before, 0, keepdims=True) + 8.0 * home_row
    after = (order_row < order_col).astype(F32)
    slot_col = jnp.sum(after, 1, keepdims=True) + 8.0 * home_col
    rank = slot_col - PAD * home_col + 1.0
    place_rank = jnp.where(place_col == iota((blocks, blocks), 1).astype(F32), rank, 0.0)
    present = dot_nn(home_hot, place_rank.astype(BF16))
    pm_send[...] = jnp.zeros_like(pm_send)
    for j in range(PAGES):
        pm_send[:, j, :] = present[:, 128 * j : 128 * (j + 1)]

    pl.semaphore_wait(barrier, n_req + 3)
    presence = (0, n_req, "req", lambda peer: pm_send.at[peer], pm_recv.at[me])
    for o in FAR:
        remote(0, o, "req", presence[3], presence[4]).start()
    pm_recv[pl.ds(me, 1)] = pm_send[pl.ds(me, 1)]

    n_slot = n_req * PAD

    len_row = lens_ref[pl.ds(me, 1), :].astype(F32)
    len_col = column(len_row)
    lane = iota((rows, 256), 1)
    frequency = jnp.exp((lane & 31).astype(F32) * (-9.210340371976184 / 32.0))
    angles = len_col * frequency
    cosines = jnp.cos(angles)
    sines = jnp.sin(angles)
    upper = (lane & 63) >= 32
    for load in loads[:4]:
        load.wait()
    values = hid[...].astype(F32)
    scale = lax.rsqrt(jnp.mean(values * values, -1, keepdims=True) + 1e-05)
    normed = (values * scale * wide_row(gain_ref)).astype(BF16)
    qk = dot_nt(normed, wqkv[pl.ds(0, 256), :])
    value_new[...] = dot_nt(normed, wqkv[pl.ds(256, 64), :]).astype(BF16)
    swapped = jnp.where(upper, pltpu.roll(qk, 32, 1), pltpu.roll(qk, 224, 1))
    turned = qk * cosines + jnp.where(upper, swapped, -swapped) * sines
    turned = jnp.where(lane < 192, turned * 0.125, turned).astype(BF16)
    rotated[...] = turned

    wait_recv_all(*presence)
    held = pm_recv[...]
    base = (iota((16, 8, 128), 0) * PAD - 1).astype(F32)
    page_slot = jnp.sum(jnp.where(held > 0.0, held + base, 0.0), 0)
    page_row = jnp.concatenate([page_slot[j : j + 1] for j in range(PAGES)], 1)
    extended = []
    for j in range(PAGES):
        used = jnp.clip(len_col - 128.0 * j, 0.0, 128.0)
        extended.append(jnp.where(lane < 192, turned.astype(F32), used).astype(BF16))
    extended = jnp.concatenate(extended, 0)

    def z_rows(oz):
        z = (mz + oz) % 4
        return z, pl.ds(pl.multiple_of(z * 4 * PAD, 4 * PAD), 4 * PAD)

    def slot_rows(index):
        return pl.ds(pl.multiple_of(index * PAD, PAD), PAD)

    queries = (1, n_req, "req", lambda peer: q_send.at[slot_rows(peer)], q_recv.at[slot_rows(me)])
    for oz in (2, 1, 3, 0):
        z, there = z_rows(oz)
        number = (iota((4 * PAD, blocks), 0) + z * 4 * PAD).astype(F32)
        pick = (number == page_row).astype(F32).astype(BF16)
        q_send[there, :] = dot_nn(pick, extended).astype(BF16)
        for ox in (2, 1, 3, 0):
            if (oz, ox) != (0, 0):
                remote(1, oz * 4 + ox, "req", queries[3], queries[4]).start()
    page_col = jnp.concatenate([column(page_slot[j : j + 1]) for j in range(PAGES)], 0)
    gather_t[...] = (iota((blocks, n_slot), 1).astype(F32) == page_col).astype(F32).astype(BF16)
    expert_row = iota((128, 16), 0)
    chosen = jnp.zeros((128, 16), F32)
    for k in range(8):
        chosen = chosen + (routes_ref[k : k + 1, :] == expert_row).astype(F32)
    eye_16 = (iota((16, 16), 0) == iota((16, 16), 1)).astype(F32).astype(BF16)
    mask_send[...] = dot_nt(eye_16, chosen.astype(BF16)).astype(BF16)
    mask_recv[0:16, :] = mask_send[...]
    each(1, n_req, lambda s: mask_copy(s).start())
    loads[6].wait()
    share_w = remote(0, 0, "core", lambda peer: wout, wout_peer)
    share_w.start()
    q_recv[slot_rows(me), :] = q_send[slot_rows(me), :]
    place_slot = (slot_col == iota((blocks, n_slot), 1).astype(F32)).astype(F32).astype(BF16)
    slot_place[...] = (iota((n_slot, blocks), 0).astype(F32) == slot_row).astype(F32).astype(BF16)
    wait_recv_all(*queries)
    arrived = dot_nn(place_slot, q_recv[...])
    zeros = jnp.zeros((blocks, HD), BF16)
    for q in range(3):
        head = arrived[:, HD * q : HD * (q + 1)].astype(BF16)
        q6[q] = jnp.concatenate([head, zeros], 1)
        q6[q + 3] = jnp.concatenate([zeros, head], 1)
    limit = arrived[:, 192:256]
    thr[...] = jnp.concatenate([limit, limit], 1)

    loads[4].wait()
    loads[5].wait()
    wide_r, wide_c = iota((96, 256), 0), iota((96, 256), 1)
    position = jnp.where((wide_r & 15) == (wide_c & 15), 2 * (wide_c >> 4), 1 << 20).astype(F32)
    stat_lane = iota((16, HD), 1)

    def some_groups(step, carry):
        at = [pl.ds(pl.multiple_of((step * 8 + k) * 16, 16), 16) for k in range(8)]
        scores = []
        for here in at:
            query = q6[:, here, :].reshape(96, 128)
            bound = thr[here, :]
            bound = jnp.concatenate([bound] * 3 + [bound - 1.0] * 3, 0)
            bound = jnp.concatenate([bound, bound], 1)
            mine = []
            for c in range(4):
                keys = jnp.concatenate(
                    [kbuf[here, 128 * i : 128 * (i + 1)] for i in range(16 * c, 16 * c + 16)], 0
                )
                mine.append(jnp.where(position < bound - 32.0 * c, dot_nt(query, keys), LOW))
            scores.append(mine)
        tops, weights, totals = [], [], []
        for mine in scores:
            top = jnp.maximum(jnp.maximum(mine[0], mine[1]), jnp.maximum(mine[2], mine[3]))
            top = jnp.max(top, 1, keepdims=True)
            top = jnp.maximum(jnp.maximum(top[:48], top[48:]), -1e29)
            top_2 = jnp.concatenate([top, top], 0)
            these = [jnp.exp(s - top_2) for s in mine]
            total = jnp.sum((these[0] + these[1]) + (these[2] + these[3]), 1, keepdims=True)
            tops.append(top)
            weights.append([w.astype(BF16) for w in these])
            totals.append(total[:48] + total[48:])
        for here, top, these, total in zip(at, tops, weights, totals):
            numer = jnp.zeros((96, 128), F32)
            for c in range(4):
                vals = jnp.concatenate(
                    [vbuf[here, 128 * i : 128 * (i + 1)] for i in range(16 * c, 16 * c + 16)], 0
                )
                numer = numer + dot_nn(these[c], vals)
            numer = numer[:48, :HD] + numer[48:, HD:]
            some = total > 0.0
            safe = jnp.where(some, total, 1.0)
            numer = numer / safe
            lse = jnp.where(some, top + jnp.log(safe), LOW)
            pieces = [numer[16 * q : 16 * (q + 1)] for q in range(3)]
            stats = jnp.zeros((16, HD), F32)
            for q in range(3):
                for t, term in enumerate(split_3(lse[16 * q : 16 * (q + 1)])):
                    stats = jnp.where(stat_lane == 16 * t + q, term, stats)
            part[here, :] = jnp.concatenate(pieces + [stats], 1).astype(BF16)
        return carry

    lax.fori_loop(0, blocks // (16 * 8), some_groups, 0)

    partials = (
        2, n_req, "req", lambda peer: part_send.at[slot_rows(peer)], part_recv.at[slot_rows(me)],
    )
    for oz in (2, 1, 3, 0):
        z, there = z_rows(oz)
        part_send[there, :] = dot_nn(slot_place[there, :], part[...]).astype(BF16)
        for ox in (2, 1, 3, 0):
            if (oz, ox) != (0, 0):
                remote(2, oz * 4 + ox, "req", partials[3], partials[4]).start()
    part_recv[slot_rows(me), :] = part_send[slot_rows(me), :]
    own_q = rotated[...].astype(F32)
    own_k = own_q[:, 192:256]
    own_v = value_new[...].astype(F32)
    own_score = [
        jnp.broadcast_to(
            jnp.sum(own_q[:, HD * q : HD * (q + 1)] * own_k, 1, keepdims=True), (rows, HD)
        )
        for q in range(3)
    ]
    own_score = jnp.concatenate(own_score + [jnp.zeros((rows, HD), F32)], 1)
    own_v = jnp.concatenate([own_v] * 4, 1)
    spread_r, spread_c = iota((HD, 256), 0), iota((HD, 256), 1)
    spread = ((spread_r & 15) == (spread_c >> 6)) & (spread_r < 48) & (spread_c < 192)
    spread = spread.astype(F32).astype(BF16)
    wait_recv_all(*partials)
    pages = dot_nn(gather_t[...], part_recv[...])
    lses = dot_nn(pages[:, 192:256].astype(BF16), spread)
    lses = [own_score] + [lses[128 * j : 128 * (j + 1)] for j in range(PAGES)]
    outs = [own_v] + [pages[128 * j : 128 * (j + 1)] for j in range(PAGES)]
    peak = jnp.maximum(jnp.maximum(lses[0], lses[1]), jnp.maximum(lses[2], lses[3]))
    shares = [jnp.exp(value - peak) for value in lses]
    whole = (shares[0] + shares[1]) + (shares[2] + shares[3])
    summed = shares[0] * outs[0] + shares[1] * outs[1]
    summed = summed + shares[2] * outs[2] + shares[3] * outs[3]
    attended = summed / whole
    attended = jnp.where(lane < 192, attended, 0.0).astype(BF16)
    att[...] = attended.reshape(4, 2, 16, 256)
    swap = remote(3, 0, "core", lambda peer: att.at[:, 1 - core], att_peer)
    swap.start()

    own_rows = att[:, pl.ds(core, 1)].reshape(64, 256)[:, :192]
    own_part = [dot_nn(own_rows, wout[:, n : n + 512]) for n in range(0, model, 512)]
    share_w.wait_recv()
    swap.wait_recv()
    peer_rows = att_peer[...].reshape(64, 256)[:, :192]
    for n in range(0, model, 512):
        part_n = own_part[n // 512] + dot_nn(peer_rows, wout_peer[:, n : n + 512])
        proj[:, :, n : n + 512] = part_n.astype(BF16).reshape(4, 16, 512)
    sums = (3, 4, "y", lambda peer: proj.at[peer // 2], proj_recv)
    start_all(*sums)
    own_proj = proj[pl.ds(kv // 2, 1)].reshape(16, model).astype(F32)
    wait_recv_all(*sums)
    after_attn = hid[token_rows(kv), :].astype(F32)
    total = own_proj
    for k in range(1, 4):
        total = total + proj_recv[k].astype(F32)
    after_attn = after_attn + total
    scale = lax.rsqrt(jnp.mean(after_attn * after_attn, -1, keepdims=True) + 1e-05)
    moe_in = (after_attn * scale * wide_row(moe_gain_ref)).astype(BF16)
    tok_send[...] = moe_in
    each(1, 7, lambda s: token_copy(s).start())
    tok[0:16, :] = tok_send[...]
    for s in range(1, 7):
        token_copy(s).wait_recv()
        for t in range(7, 16):
            oz, ox = ORDER[t]
            ready = {1: [(1, 1)], 2: [(3, 3)], 3: [(1, 3)], 4: [(3, 1)], 5: [(1, 2), (3, 2)]}
            if (oz, ox) in ready.get(s, [(2, 1), (2, 3), (2, 2)]):
                token_copy(t).start()
    loads[7].wait()
    loads[8].wait()
    each(1, n_req, lambda s: mask_copy(s).wait_recv())
    for first, last in CHUNKS:
        each(max(first, 7), last, lambda s: token_copy(s).wait_recv())
        count = 16 * (last - first)
        here = pl.ds(16 * first, count)
        gate_lane = iota((count, 128), 1)
        inputs = tok[here, :]
        logits = jnp.concatenate([dot_nt(inputs, router_ref[...])] * 4, 1)
        logits = jnp.where(mask_recv[here, :].astype(F32) > 0.0, logits, LOW)
        gates = jnp.exp(logits - jnp.max(logits, 1, keepdims=True))
        gates = gates / jnp.sum(gates, 1, keepdims=True)
        for e in range(2):
            weight = jnp.sum(jnp.where(gate_lane == 2 * me + e, gates, 0.0), 1, keepdims=True)
            acts = []
            for f in range(0, FFE, 256):
                gate = dot_nn(inputs, up[e, :, f : f + 256])
                lift = dot_nn(inputs, up[e, :, FFE + f : FFE + f + 256])
                acts.append((gate * jax.nn.sigmoid(gate) * lift).astype(BF16))
            act = jnp.concatenate(acts, 1)
            for n in range(0, model, 256):
                made = dot_nn(act, down[e, :, n : n + 256]).astype(BF16).astype(F32) * weight
                if e == 0:
                    mixed[0:count, n : n + 256] = made
                else:
                    made = mixed[0:count, n : n + 256] + made
                    mixed_send[here, n : n + 256] = made.astype(BF16)
        each(max(first, 1), last, lambda s: back_copy(s).start())

    result = mixed_send[0:16, :].astype(F32)
    for d in range(1, n_req):
        back_copy(d).wait_recv()
        result = result + mixed_recv[d].astype(F32)
    out_ref[...] = (after_attn + result).astype(BF16)
    each(1, n_req, lambda s: mask_copy(s).wait_send())
    each(1, n_req, lambda s: token_copy(s).wait_send())
    each(1, n_req, lambda s: back_copy(s).wait_send())
    share_w.wait_send()
    swap.wait_send()
    for exchange in (presence, queries, partials, sums):
        wait_send_all(*exchange)


def shards(
    hidden_in, attn_gain, w_query, w_key, w_value, w_out, k_cache, v_cache, cache_len, block_slot,
    moe_gain, w_router, w_gate_up, w_down, routes,
):
    any_spec = pl.BlockSpec(memory_space=pl.ANY)
    vmem = pl.BlockSpec(memory_space=pltpu.VMEM)
    blocks = k_cache.shape[0]
    model = hidden_in.shape[1]
    rows = hidden_in.shape[0]
    n_slot = 16 * PAD
    scratch = [
        ((rows, model), BF16), ((320, model), BF16), ((192, model), BF16),
        ((blocks, 8192), BF16), ((blocks, 8192), BF16),
        (w_gate_up.shape, BF16), (w_down.shape, BF16),
        ((16, 8, 128), F32), ((16, 8, 128), F32),
        ((n_slot, 256), BF16), ((n_slot, 256), BF16),
        ((6, blocks, 128), BF16), ((blocks, 128), F32),
        ((blocks, 256), BF16), ((n_slot, 256), BF16), ((n_slot, 256), BF16),
        ((blocks, n_slot), BF16),
        ((rows, 256), BF16), ((rows, HD), BF16), ((4, 16, model), BF16), ((4, 16, model), BF16),
        ((4, 2, 16, 256), BF16), ((4, 16, 256), BF16), ((192, model), BF16),
        ((16, 128), BF16), ((256, 128), BF16), ((n_slot, blocks), BF16),
        ((16, model), BF16), ((256, model), BF16),
        ((80, model), F32), ((256, model), BF16), ((16, 16, model), BF16),
    ]
    return pl.pallas_call(
        kernel,
        out_shape=jax.ShapeDtypeStruct((16, model), BF16),
        in_specs=[
            any_spec, vmem, any_spec, any_spec, any_spec, any_spec, any_spec, any_spec, vmem, vmem,
            vmem, vmem, any_spec, any_spec, vmem,
        ],
        out_specs=vmem,
        scratch_shapes=[pltpu.VMEM(shape, dtype) for shape, dtype in scratch]
        + [
            pltpu.SemaphoreType.DMA((9,)),
            pltpu.SemaphoreType.DMA((7, 16)),
            pltpu.SemaphoreType.DMA((7, 16)),
        ],
        compiler_params=pltpu.CompilerParams(
            collective_id=0, has_side_effects=True, vmem_limit_bytes=56 << 20
        ),
    )(
        hidden_in, attn_gain.reshape(model // 128, 128), w_query, w_key, w_value, w_out,
        k_cache.reshape(blocks, 8192), v_cache.reshape(blocks, 8192),
        cache_len.reshape(16, 128), block_slot.reshape(3, 128),
        moe_gain.reshape(model // 128, 128), w_router.T, w_gate_up, w_down, routes.T,
    )


def solution(mesh):
    placed = (
        P("req", None),
        P(),
        P("kv", None),
        P("kv", None),
        P("kv", None),
        P("kv", None),
        P("req", "kv", None),
        P("req", "kv", None),
        P(),
        P("req"),
        P(),
        P(),
        P("req", None, None),
        P("req", None, None),
        P(("req", "kv"), None),
    )
    return jax.shard_map(
        shards, mesh=mesh, in_specs=placed, out_specs=P(("req", "kv"), None), check_vma=False
    )
```

```python
import jax
import jax.numpy as jnp
from jax import lax
from jax.experimental import pallas as pl
from jax.experimental.pallas import tpu as pltpu
from jax.sharding import PartitionSpec as P

HD = 64
FFE = 512
BLK = 128
PAGES = 3
PAD = 32
SHARE = 24
ORDER = [
    (0, 0), (0, 2), (2, 0), (0, 1), (0, 3), (1, 0), (3, 0),
    (1, 1), (3, 3), (1, 3), (3, 1), (1, 2), (3, 2), (2, 1), (2, 3), (2, 2),
]
FAR = [oz * 4 + ox for oz, ox in reversed(ORDER) if (oz, ox) != (0, 0)]
CHUNKS = [(0, 7), (7, 11), (11, 16)]
DIRECT = 11
X_FIRST = [(1, 2), (3, 2)]
LOW = -1e30
MESH = pl.DeviceIdType.MESH
F32 = jnp.float32
BF16 = jnp.bfloat16


def dot_nt(left, right):
    return lax.dot_general(left, right, (((1,), (1,)), ((), ())), preferred_element_type=F32)


def dot_nn(left, right):
    return jnp.dot(left, right, preferred_element_type=F32)


def iota(shape, axis):
    return lax.broadcasted_iota(jnp.int32, shape, axis)


def split_3(value):
    high = value.astype(BF16).astype(F32)
    rest = value - high
    middle = rest.astype(BF16).astype(F32)
    return high, middle, rest - middle


def kernel(
    hidden_hbm, gain_hbm, wq_hbm, wk_hbm, wv_hbm, wout_hbm, k_hbm, v_hbm, lens_hbm, slots_hbm,
    moe_gain_hbm, router_hbm, up_hbm, down_hbm, routes_hbm,
    out_ref,
    gain_ref, lens_ref, slots_ref, moe_gain_ref, router_ref, routes_ref,
    hid, wqkv, wout, kbuf, vbuf, up, down,
    pm_send, pm_recv, q_send, q_recv, q6, thr, part, part_send, part_recv, gather_t,
    rotated, value_new, proj, proj_recv, att, att_peer, wout_peer,
    mask_send, mask_recv, slot_place, tok_send, tok, mixed, mixed_send, mixed_recv,
    local_sem, send_sem, recv_sem,
):
    me = lax.axis_index("req")
    kv = lax.axis_index("kv")
    mz, mx = me // 4, me % 4
    n_req, n_kv = 16, 8
    rows, model = hid.shape
    blocks = kbuf.shape[0]

    def req_peer(o):
        return ((mz + o // 4) % 4) * 4 + (mx + o % 4) % 4

    barrier = pltpu.get_barrier_semaphore()

    for o in FAR:
        pl.semaphore_signal(barrier, inc=1, device_id={"req": req_peer(o)}, device_id_type=MESH)

    def greet_kv(o, carry):
        peer = (kv + 2 * o) % n_kv
        pl.semaphore_signal(barrier, inc=1, device_id={"kv": peer}, device_id_type=MESH)
        return carry

    lax.fori_loop(1, 4, greet_kv, 0)
    pl.semaphore_signal(
        barrier, inc=1, device_id={"kv": kv + 1 - 2 * (kv % 2)}, device_id_type=MESH
    )

    loads = [
        (hidden_hbm, hid), (wq_hbm, wqkv.at[pl.ds(0, 192)]), (wk_hbm, wqkv.at[pl.ds(192, 64)]),
        (wv_hbm, wqkv.at[pl.ds(256, 64)]), (k_hbm, kbuf), (v_hbm, vbuf), (wout_hbm, wout),
        (up_hbm, up), (down_hbm, down),
    ]
    loads = [
        pltpu.make_async_copy(src, dst, local_sem.at[i]) for i, (src, dst) in enumerate(loads)
    ]
    smalls = [
        (slots_hbm, slots_ref), (lens_hbm, lens_ref), (gain_hbm, gain_ref),
        (moe_gain_hbm, moe_gain_ref), (router_hbm, router_ref), (routes_hbm, routes_ref),
    ]
    smalls = [
        pltpu.make_async_copy(src, dst, local_sem.at[9 + i]) for i, (src, dst) in enumerate(smalls)
    ]
    for load in smalls + loads[:7]:
        load.start()
    for load in smalls:
        load.wait()

    def remote(phase, o, axis, source, target):
        if axis == "req":
            name, peer = "req", req_peer(o)
        elif axis == "core":
            name, peer = "kv", kv + 1 - 2 * (kv % 2)
        else:
            name, peer = "kv", (kv + 2 * o) % n_kv
        if axis == "y":
            target = target.at[o]
        return pltpu.make_async_remote_copy(
            src_ref=source(peer), dst_ref=target, send_sem=send_sem.at[phase, o],
            recv_sem=recv_sem.at[phase, o], device_id={name: peer}, device_id_type=MESH,
        )

    def far_req(s):
        oz, ox = ORDER[s]
        return ((mz + oz) % 4) * 4 + (mx + ox) % 4

    def near_req(s):
        oz, ox = ORDER[s]
        return ((mz + 4 - oz) % 4) * 4 + (mx + 4 - ox) % 4

    def token_rows(index):
        return pl.ds(pl.multiple_of(index * 16, 16), 16)

    def slot_copy(phase, s, source, target, peer):
        return pltpu.make_async_remote_copy(
            src_ref=source, dst_ref=target, send_sem=send_sem.at[phase, s],
            recv_sem=recv_sem.at[phase, s], device_id={"req": peer}, device_id_type=MESH,
        )

    def mask_copy(s):
        return slot_copy(6, s, mask_send, mask_recv.at[pl.ds(16 * s, 16)], far_req(s))

    core = kv % 2

    def token_copy(s):
        oz, ox = ORDER[s]
        if s < DIRECT:
            source, peer = tok_send, far_req(s)
        else:
            by_x, by_z = ORDER.index((0, ox)), ORDER.index((oz, 0))
            to_z = ((mz + oz) % 4) * 4 + mx
            to_x = mz * 4 + (mx + ox) % 4
            if (oz, ox) == (2, 2):
                source = tok.at[token_rows(by_x + core * (by_z - by_x))]
                peer = to_z + core * (to_x - to_z)
            elif (oz, ox) in X_FIRST:
                source, peer = tok.at[token_rows(by_x)], to_z
            else:
                source, peer = tok.at[token_rows(by_z)], to_x
        return slot_copy(4, s, source, tok.at[token_rows(s)], peer)

    def back_copy(s):
        return slot_copy(5, s, mixed_send.at[pl.ds(16 * s, 16)], mixed_recv.at[s], near_req(s))

    def each(first, last, action):
        for s in range(first, last):
            action(s)

    def start_all(phase, count, axis, source, target):
        def body(o, carry):
            remote(phase, o, axis, source, target).start()
            return carry

        lax.fori_loop(1, count, body, 0)

    def wait_recv_all(phase, count, axis, source, target):
        def body(o, carry):
            remote(phase, o, axis, source, target).wait_recv()
            return carry

        lax.fori_loop(1, count, body, 0)

    def wait_send_all(phase, count, axis, source, target):
        def body(o, carry):
            remote(phase, o, axis, source, target).wait_send()
            return carry

        lax.fori_loop(1, count, body, 0)

    eye = iota((128, 128), 0) == iota((128, 128), 1)

    def column(row):
        return jnp.sum(jnp.where(eye, row, 0.0), 1, keepdims=True)

    def wide_row(ref):
        return jnp.concatenate([ref[i : i + 1, :] for i in range(ref.shape[0])], 1)

    slots = slots_ref[...]
    owner = (slots * 43691) >> 17
    page = slots - owner * PAGES
    home = owner >> 7
    place = page * 128 + (owner & 127)
    home_f = home.astype(F32)
    place_f = place.astype(F32)
    home_row = jnp.concatenate([home_f[i : i + 1] for i in range(3)], 1)
    place_row = jnp.concatenate([place_f[i : i + 1] for i in range(3)], 1)
    home_col = jnp.concatenate([column(home_f[i : i + 1]) for i in range(3)], 0)
    place_col = jnp.concatenate([column(place_f[i : i + 1]) for i in range(3)], 0)
    home_hot = (home_row == iota((16, blocks), 0).astype(F32)).astype(F32).astype(BF16)
    order_row = home_row * 384.0 + place_row
    order_col = home_col * 384.0 + place_col
    before = (order_col < order_row).astype(F32)
    slot_row = jnp.sum(before, 0, keepdims=True) + 8.0 * home_row
    after = (order_row < order_col).astype(F32)
    slot_col = jnp.sum(after, 1, keepdims=True) + 8.0 * home_col
    rank = slot_col - PAD * home_col + 1.0
    place_rank = jnp.where(place_col == iota((blocks, blocks), 1).astype(F32), rank, 0.0)
    present = dot_nn(home_hot, place_rank.astype(BF16))
    pm_send[...] = jnp.zeros_like(pm_send)
    q_recv[...] = jnp.zeros_like(q_recv)
    part_recv[...] = jnp.zeros_like(part_recv)
    for j in range(PAGES):
        pm_send[:, j, :] = present[:, 128 * j : 128 * (j + 1)]

    pl.semaphore_wait(barrier, n_req + 3)
    presence = (0, n_req, "req", lambda peer: pm_send.at[peer], pm_recv.at[me])
    for o in FAR:
        remote(0, o, "req", presence[3], presence[4]).start()
    pm_recv[pl.ds(me, 1)] = pm_send[pl.ds(me, 1)]

    n_slot = n_req * PAD

    len_row = lens_ref[pl.ds(me, 1), :].astype(F32)
    len_col = column(len_row)
    lane = iota((rows, 256), 1)
    frequency = jnp.exp((lane & 31).astype(F32) * (-9.210340371976184 / 32.0))
    angles = len_col * frequency
    cosines = jnp.cos(angles)
    sines = jnp.sin(angles)
    upper = (lane & 63) >= 32
    for load in loads[:4]:
        load.wait()
    values = hid[...].astype(F32)
    scale = lax.rsqrt(jnp.mean(values * values, -1, keepdims=True) + 1e-05)
    normed = (values * scale * wide_row(gain_ref)).astype(BF16)
    qk = dot_nt(normed, wqkv[pl.ds(0, 256), :])
    value_new[...] = dot_nt(normed, wqkv[pl.ds(256, 64), :]).astype(BF16)
    swapped = jnp.where(upper, pltpu.roll(qk, 32, 1), pltpu.roll(qk, 224, 1))
    turned = qk * cosines + jnp.where(upper, swapped, -swapped) * sines
    turned = jnp.where(lane < 192, turned * 0.125, turned).astype(BF16)
    rotated[...] = turned

    wait_recv_all(*presence)
    held = pm_recv[...]
    base = (iota((16, 8, 128), 0) * PAD - 1).astype(F32)
    page_slot = jnp.sum(jnp.where(held > 0.0, held + base, 0.0), 0)
    page_row = jnp.concatenate([page_slot[j : j + 1] for j in range(PAGES)], 1)
    extended = []
    for j in range(PAGES):
        used = jnp.clip(len_col - 128.0 * j, 0.0, 128.0)
        extended.append(jnp.where(lane < 192, turned.astype(F32), used).astype(BF16))
    extended = jnp.concatenate(extended, 0)

    def z_rows(oz):
        z = (mz + oz) % 4
        return z, pl.ds(pl.multiple_of(z * 4 * PAD, 4 * PAD), 4 * PAD)

    def slot_rows(index):
        return pl.ds(pl.multiple_of(index * PAD, PAD), SHARE)

    queries = (1, n_req, "req", lambda peer: q_send.at[slot_rows(peer)], q_recv.at[slot_rows(me)])
    for oz in (2, 1, 3, 0):
        z, there = z_rows(oz)
        number = (iota((4 * PAD, blocks), 0) + z * 4 * PAD).astype(F32)
        pick = (number == page_row).astype(F32).astype(BF16)
        q_send[there, :] = dot_nn(pick, extended).astype(BF16)
        for ox in (2, 1, 3, 0):
            if (oz, ox) != (0, 0):
                remote(1, oz * 4 + ox, "req", queries[3], queries[4]).start()
    page_col = jnp.concatenate([column(page_slot[j : j + 1]) for j in range(PAGES)], 0)
    gather_t[...] = (iota((blocks, n_slot), 1).astype(F32) == page_col).astype(F32).astype(BF16)
    expert_row = iota((128, 16), 0)
    chosen = jnp.zeros((128, 16), F32)
    for k in range(8):
        chosen = chosen + (routes_ref[k : k + 1, :] == expert_row).astype(F32)
    eye_16 = (iota((16, 16), 0) == iota((16, 16), 1)).astype(F32).astype(BF16)
    mask_send[...] = dot_nt(eye_16, chosen.astype(BF16)).astype(BF16)
    mask_recv[0:16, :] = mask_send[...]
    each(1, n_req, lambda s: mask_copy(s).start())
    loads[7].start()
    loads[8].start()
    loads[6].wait()
    share_w = remote(0, 0, "core", lambda peer: wout, wout_peer)
    share_w.start()
    q_recv[slot_rows(me), :] = q_send[slot_rows(me), :]
    place_slot = (slot_col == iota((blocks, n_slot), 1).astype(F32)).astype(F32).astype(BF16)
    slot_place[...] = (iota((n_slot, blocks), 0).astype(F32) == slot_row).astype(F32).astype(BF16)
    wait_recv_all(*queries)
    arrived = dot_nn(place_slot, q_recv[...])
    zeros = jnp.zeros((blocks, HD), BF16)
    for q in range(3):
        head = arrived[:, HD * q : HD * (q + 1)].astype(BF16)
        q6[q] = jnp.concatenate([head, zeros], 1)
        q6[q + 3] = jnp.concatenate([zeros, head], 1)
    limit = arrived[:, 192:256]
    thr[...] = jnp.concatenate([limit, limit], 1)

    loads[4].wait()
    loads[5].wait()
    wide_r, wide_c = iota((96, 256), 0), iota((96, 256), 1)
    position = jnp.where((wide_r & 15) == (wide_c & 15), 2 * (wide_c >> 4), 1 << 20).astype(F32)
    stat_lane = iota((16, HD), 1)

    def some_groups(step, carry):
        at = [pl.ds(pl.multiple_of((step * 8 + k) * 16, 16), 16) for k in range(8)]
        scores = []
        for here in at:
            query = q6[:, here, :].reshape(96, 128)
            bound = thr[here, :]
            bound = jnp.concatenate([bound] * 3 + [bound - 1.0] * 3, 0)
            bound = jnp.concatenate([bound, bound], 1)
            mine = []
            for c in range(4):
                keys = jnp.concatenate(
                    [kbuf[here, 128 * i : 128 * (i + 1)] for i in range(16 * c, 16 * c + 16)], 0
                )
                mine.append(jnp.where(position < bound - 32.0 * c, dot_nt(query, keys), LOW))
            scores.append(mine)
        tops, weights, totals = [], [], []
        for mine in scores:
            top = jnp.maximum(jnp.maximum(mine[0], mine[1]), jnp.maximum(mine[2], mine[3]))
            top = jnp.max(top, 1, keepdims=True)
            top = jnp.maximum(jnp.maximum(top[:48], top[48:]), -1e29)
            top_2 = jnp.concatenate([top, top], 0)
            these = [jnp.exp(s - top_2) for s in mine]
            total = jnp.sum((these[0] + these[1]) + (these[2] + these[3]), 1, keepdims=True)
            tops.append(top)
            weights.append([w.astype(BF16) for w in these])
            totals.append(total[:48] + total[48:])
        for here, top, these, total in zip(at, tops, weights, totals):
            numer = jnp.zeros((96, 128), F32)
            for c in range(4):
                vals = jnp.concatenate(
                    [vbuf[here, 128 * i : 128 * (i + 1)] for i in range(16 * c, 16 * c + 16)], 0
                )
                numer = numer + dot_nn(these[c], vals)
            numer = numer[:48, :HD] + numer[48:, HD:]
            some = total > 0.0
            safe = jnp.where(some, total, 1.0)
            numer = numer / safe
            lse = jnp.where(some, top + jnp.log(safe), LOW)
            pieces = [numer[16 * q : 16 * (q + 1)] for q in range(3)]
            stats = jnp.zeros((16, HD), F32)
            for q in range(3):
                for t, term in enumerate(split_3(lse[16 * q : 16 * (q + 1)])):
                    stats = jnp.where(stat_lane == 16 * t + q, term, stats)
            part[here, :] = jnp.concatenate(pieces + [stats], 1).astype(BF16)
        return carry

    lax.fori_loop(0, blocks // (16 * 8), some_groups, 0)

    partials = (
        2, n_req, "req", lambda peer: part_send.at[slot_rows(peer)], part_recv.at[slot_rows(me)],
    )
    for oz in (2, 1, 3, 0):
        z, there = z_rows(oz)
        part_send[there, :] = dot_nn(slot_place[there, :], part[...]).astype(BF16)
        for ox in (2, 1, 3, 0):
            if (oz, ox) != (0, 0):
                remote(2, oz * 4 + ox, "req", partials[3], partials[4]).start()
    part_recv[slot_rows(me), :] = part_send[slot_rows(me), :]
    own_q = rotated[...].astype(F32)
    own_k = own_q[:, 192:256]
    own_v = value_new[...].astype(F32)
    own_score = [
        jnp.broadcast_to(
            jnp.sum(own_q[:, HD * q : HD * (q + 1)] * own_k, 1, keepdims=True), (rows, HD)
        )
        for q in range(3)
    ]
    own_score = jnp.concatenate(own_score + [jnp.zeros((rows, HD), F32)], 1)
    own_v = jnp.concatenate([own_v] * 4, 1)
    spread_r, spread_c = iota((HD, 256), 0), iota((HD, 256), 1)
    spread = ((spread_r & 15) == (spread_c >> 6)) & (spread_r < 48) & (spread_c < 192)
    spread = spread.astype(F32).astype(BF16)
    wait_recv_all(*partials)
    pages = dot_nn(gather_t[...], part_recv[...])
    lses = dot_nn(pages[:, 192:256].astype(BF16), spread)
    lses = [own_score] + [lses[128 * j : 128 * (j + 1)] for j in range(PAGES)]
    outs = [own_v] + [pages[128 * j : 128 * (j + 1)] for j in range(PAGES)]
    peak = jnp.maximum(jnp.maximum(lses[0], lses[1]), jnp.maximum(lses[2], lses[3]))
    shares = [jnp.exp(value - peak) for value in lses]
    whole = (shares[0] + shares[1]) + (shares[2] + shares[3])
    summed = shares[0] * outs[0] + shares[1] * outs[1]
    summed = summed + shares[2] * outs[2] + shares[3] * outs[3]
    attended = summed / whole
    attended = jnp.where(lane < 192, attended, 0.0).astype(BF16)
    att[...] = attended.reshape(4, 2, 16, 256)
    swap = remote(3, 0, "core", lambda peer: att.at[:, 1 - core], att_peer)
    swap.start()

    own_rows = att[:, pl.ds(core, 1)].reshape(64, 256)[:, :192]
    own_part = [dot_nn(own_rows, wout[:, n : n + 512]) for n in range(0, model, 512)]
    share_w.wait_recv()
    swap.wait_recv()
    peer_rows = att_peer[...].reshape(64, 256)[:, :192]
    for n in range(0, model, 512):
        part_n = own_part[n // 512] + dot_nn(peer_rows, wout_peer[:, n : n + 512])
        proj[:, :, n : n + 512] = part_n.astype(BF16).reshape(4, 16, 512)
    sums = (3, 4, "y", lambda peer: proj.at[peer // 2], proj_recv)
    start_all(*sums)
    own_proj = proj[pl.ds(kv // 2, 1)].reshape(16, model).astype(F32)
    wait_recv_all(*sums)
    after_attn = hid[token_rows(kv), :].astype(F32)
    total = own_proj
    for k in range(1, 4):
        total = total + proj_recv[k].astype(F32)
    after_attn = after_attn + total
    scale = lax.rsqrt(jnp.mean(after_attn * after_attn, -1, keepdims=True) + 1e-05)
    moe_in = (after_attn * scale * wide_row(moe_gain_ref)).astype(BF16)
    tok_send[...] = moe_in
    each(1, DIRECT, lambda s: token_copy(s).start())
    tok[0:16, :] = tok_send[...]
    for s, onward in ((1, [(1, 2), (3, 2)]), (2, [(2, 1), (2, 3), (2, 2)])):
        token_copy(s).wait_recv()
        for place in onward:
            token_copy(ORDER.index(place)).start()
    loads[7].wait()
    loads[8].wait()
    each(1, n_req, lambda s: mask_copy(s).wait_recv())
    for first, last in CHUNKS:
        each(max(first, 3), last, lambda s: token_copy(s).wait_recv())
        count = 16 * (last - first)
        here = pl.ds(16 * first, count)
        gate_lane = iota((count, 128), 1)
        inputs = tok[here, :]
        logits = jnp.concatenate([dot_nt(inputs, router_ref[...])] * 4, 1)
        logits = jnp.where(mask_recv[here, :].astype(F32) > 0.0, logits, LOW)
        gates = jnp.exp(logits - jnp.max(logits, 1, keepdims=True))
        gates = gates / jnp.sum(gates, 1, keepdims=True)
        for e in range(2):
            weight = jnp.sum(jnp.where(gate_lane == 2 * me + e, gates, 0.0), 1, keepdims=True)
            acts = []
            for f in range(0, FFE, 256):
                gate = dot_nn(inputs, up[e, :, f : f + 256])
                lift = dot_nn(inputs, up[e, :, FFE + f : FFE + f + 256])
                acts.append((gate * jax.nn.sigmoid(gate) * lift).astype(BF16))
            act = jnp.concatenate(acts, 1)
            for n in range(0, model, 256):
                made = dot_nn(act, down[e, :, n : n + 256]).astype(BF16).astype(F32) * weight
                if e == 0:
                    mixed[0:count, n : n + 256] = made
                else:
                    made = mixed[0:count, n : n + 256] + made
                    mixed_send[here, n : n + 256] = made.astype(BF16)
        each(max(first, 1), last, lambda s: back_copy(s).start())

    result = mixed_send[0:16, :].astype(F32)
    for d in range(1, n_req):
        back_copy(d).wait_recv()
        result = result + mixed_recv[d].astype(F32)
    out_ref[...] = (after_attn + result).astype(BF16)
    each(1, n_req, lambda s: mask_copy(s).wait_send())
    each(1, n_req, lambda s: token_copy(s).wait_send())
    each(1, n_req, lambda s: back_copy(s).wait_send())
    share_w.wait_send()
    swap.wait_send()
    for exchange in (presence, queries, partials, sums):
        wait_send_all(*exchange)


def shards(
    hidden_in, attn_gain, w_query, w_key, w_value, w_out, k_cache, v_cache, cache_len, block_slot,
    moe_gain, w_router, w_gate_up, w_down, routes,
):
    any_spec = pl.BlockSpec(memory_space=pl.ANY)
    vmem = pl.BlockSpec(memory_space=pltpu.VMEM)
    blocks = k_cache.shape[0]
    model = hidden_in.shape[1]
    rows = hidden_in.shape[0]
    n_slot = 16 * PAD
    scratch = [
        ((rows, model), BF16), ((320, model), BF16), ((192, model), BF16),
        ((blocks, 8192), BF16), ((blocks, 8192), BF16),
        (w_gate_up.shape, BF16), (w_down.shape, BF16),
        ((16, 8, 128), F32), ((16, 8, 128), F32),
        ((n_slot, 256), BF16), ((n_slot, 256), BF16),
        ((6, blocks, 128), BF16), ((blocks, 128), F32),
        ((blocks, 256), BF16), ((n_slot, 256), BF16), ((n_slot, 256), BF16),
        ((blocks, n_slot), BF16),
        ((rows, 256), BF16), ((rows, HD), BF16), ((4, 16, model), BF16), ((4, 16, model), BF16),
        ((4, 2, 16, 256), BF16), ((4, 16, 256), BF16), ((192, model), BF16),
        ((16, 128), BF16), ((256, 128), BF16), ((n_slot, blocks), BF16),
        ((16, model), BF16), ((256, model), BF16),
        ((112, model), F32), ((256, model), BF16), ((16, 16, model), BF16),
    ]
    return pl.pallas_call(
        kernel,
        out_shape=jax.ShapeDtypeStruct((16, model), BF16),
        in_specs=[any_spec] * 15,
        out_specs=vmem,
        scratch_shapes=[
            pltpu.VMEM((model // 128, 128), F32), pltpu.VMEM((16, 128), jnp.int32),
            pltpu.VMEM((3, 128), jnp.int32), pltpu.VMEM((model // 128, 128), F32),
            pltpu.VMEM((32, model), BF16), pltpu.VMEM((8, 16), jnp.int32),
        ]
        + [pltpu.VMEM(shape, dtype) for shape, dtype in scratch]
        + [
            pltpu.SemaphoreType.DMA((15,)),
            pltpu.SemaphoreType.DMA((7, 16)),
            pltpu.SemaphoreType.DMA((7, 16)),
        ],
        compiler_params=pltpu.CompilerParams(
            collective_id=0, has_side_effects=True, vmem_limit_bytes=56 << 20
        ),
    )(
        hidden_in, attn_gain.reshape(model // 128, 128), w_query, w_key, w_value, w_out,
        k_cache.reshape(blocks, 8192), v_cache.reshape(blocks, 8192),
        cache_len.reshape(16, 128), block_slot.reshape(3, 128),
        moe_gain.reshape(model // 128, 128), w_router.T, w_gate_up, w_down, routes.T,
    )


def solution(mesh):
    placed = (
        P("req", None),
        P(),
        P("kv", None),
        P("kv", None),
        P("kv", None),
        P("kv", None),
        P("req", "kv", None),
        P("req", "kv", None),
        P(),
        P("req"),
        P(),
        P(),
        P("req", None, None),
        P("req", None, None),
        P(("req", "kv"), None),
    )
    return jax.shard_map(
        shards, mesh=mesh, in_specs=placed, out_specs=P(("req", "kv"), None), check_vma=False
    )
```

```python
import jax
import jax.numpy as jnp
from jax import lax
from jax.experimental import pallas as pl
from jax.experimental.pallas import tpu as pltpu
from jax.sharding import PartitionSpec as P

HD = 64
FFE = 512
BLK = 128
PAGES = 3
PAD = 32
SHARE = 24
ORDER = [
    (0, 0), (0, 2), (2, 0), (0, 1), (0, 3), (1, 0), (3, 0),
    (1, 1), (3, 3), (1, 3), (3, 1), (1, 2), (3, 2), (2, 1), (2, 3), (2, 2),
]
FAR = [oz * 4 + ox for oz, ox in reversed(ORDER) if (oz, ox) != (0, 0)]
CHUNKS = [(0, 7), (7, 11), (11, 16)]
DIRECT = 11
SPLIT = 7
X_FIRST = [(1, 2), (3, 2)]
LOW = -1e30
MESH = pl.DeviceIdType.MESH
F32 = jnp.float32
BF16 = jnp.bfloat16


def dot_nt(left, right):
    return lax.dot_general(left, right, (((1,), (1,)), ((), ())), preferred_element_type=F32)


def dot_nn(left, right):
    return jnp.dot(left, right, preferred_element_type=F32)


def iota(shape, axis):
    return lax.broadcasted_iota(jnp.int32, shape, axis)


def split_3(value):
    high = value.astype(BF16).astype(F32)
    rest = value - high
    middle = rest.astype(BF16).astype(F32)
    return high, middle, rest - middle


def kernel(
    hidden_hbm, gain_hbm, wq_hbm, wk_hbm, wv_hbm, wout_hbm, k_hbm, v_hbm, lens_hbm, slots_hbm,
    moe_gain_hbm, router_hbm, up_hbm, down_hbm, routes_hbm,
    out_ref,
    gain_ref, lens_ref, slots_ref, moe_gain_ref, router_ref, routes_ref,
    hid, wqkv, wout, kbuf, vbuf, up, down,
    pm_send, pm_recv, q_send, q_recv, q6, thr, part, part_send, part_recv, gather_t,
    rotated, value_new, proj, proj_recv, att, att_peer, wout_peer,
    mask_send, mask_recv, slot_place, tok_send, tok, mixed_send, mixed_recv,
    local_sem, send_sem, recv_sem,
):
    me = lax.axis_index("req")
    kv = lax.axis_index("kv")
    mz, mx = me // 4, me % 4
    n_req, n_kv = 16, 8
    rows, model = hid.shape
    blocks = kbuf.shape[0]

    def req_peer(o):
        return ((mz + o // 4) % 4) * 4 + (mx + o % 4) % 4

    barrier = pltpu.get_barrier_semaphore()

    for o in FAR:
        pl.semaphore_signal(barrier, inc=1, device_id={"req": req_peer(o)}, device_id_type=MESH)

    def greet_kv(o, carry):
        peer = (kv + 2 * o) % n_kv
        pl.semaphore_signal(barrier, inc=1, device_id={"kv": peer}, device_id_type=MESH)
        return carry

    lax.fori_loop(1, 4, greet_kv, 0)
    pl.semaphore_signal(
        barrier, inc=1, device_id={"kv": kv + 1 - 2 * (kv % 2)}, device_id_type=MESH
    )

    loads = [
        (hidden_hbm, hid), (wq_hbm, wqkv.at[pl.ds(0, 192)]), (wk_hbm, wqkv.at[pl.ds(192, 64)]),
        (wv_hbm, wqkv.at[pl.ds(256, 64)]), (k_hbm, kbuf), (v_hbm, vbuf), (wout_hbm, wout),
        (up_hbm, up), (down_hbm, down),
    ]
    loads = [
        pltpu.make_async_copy(src, dst, local_sem.at[i]) for i, (src, dst) in enumerate(loads)
    ]
    smalls = [
        (slots_hbm, slots_ref), (lens_hbm, lens_ref), (gain_hbm, gain_ref),
        (moe_gain_hbm, moe_gain_ref), (router_hbm, router_ref), (routes_hbm, routes_ref),
    ]
    smalls = [
        pltpu.make_async_copy(src, dst, local_sem.at[9 + i]) for i, (src, dst) in enumerate(smalls)
    ]
    for load in smalls + loads[:7]:
        load.start()
    for load in smalls:
        load.wait()

    def remote(phase, o, axis, source, target):
        if axis == "req":
            name, peer = "req", req_peer(o)
        elif axis == "core":
            name, peer = "kv", kv + 1 - 2 * (kv % 2)
        else:
            name, peer = "kv", (kv + 2 * o) % n_kv
        if axis == "y":
            target = target.at[o]
        return pltpu.make_async_remote_copy(
            src_ref=source(peer), dst_ref=target, send_sem=send_sem.at[phase, o],
            recv_sem=recv_sem.at[phase, o], device_id={name: peer}, device_id_type=MESH,
        )

    def far_req(s):
        oz, ox = ORDER[s]
        return ((mz + oz) % 4) * 4 + (mx + ox) % 4

    def near_req(s):
        oz, ox = ORDER[s]
        return ((mz + 4 - oz) % 4) * 4 + (mx + 4 - ox) % 4

    def token_rows(index):
        return pl.ds(pl.multiple_of(index * 16, 16), 16)

    def slot_copy(phase, s, source, target, peer):
        return pltpu.make_async_remote_copy(
            src_ref=source, dst_ref=target, send_sem=send_sem.at[phase, s],
            recv_sem=recv_sem.at[phase, s], device_id={"req": peer}, device_id_type=MESH,
        )

    def mask_copy(s):
        return slot_copy(6, s, mask_send, mask_recv.at[pl.ds(16 * s, 16)], far_req(s))

    core = kv % 2
    half = model // 2

    def half_back(s, h):
        lanes = pl.ds(half * h, half)
        return slot_copy(
            5 + 2 * h, s, mixed_send.at[pl.ds(16 * s, 16), lanes], mixed_recv.at[s, :, lanes],
            near_req(s),
        )

    def back_copies(s):
        return [half_back(s, 0), half_back(s, 1)] if s >= SPLIT else [back_copy(s)]

    def token_copy(s):
        oz, ox = ORDER[s]
        if s < DIRECT:
            source, peer = tok_send, far_req(s)
        else:
            by_x, by_z = ORDER.index((0, ox)), ORDER.index((oz, 0))
            to_z = ((mz + oz) % 4) * 4 + mx
            to_x = mz * 4 + (mx + ox) % 4
            if (oz, ox) == (2, 2):
                source = tok.at[token_rows(by_x + core * (by_z - by_x))]
                peer = to_z + core * (to_x - to_z)
            elif (oz, ox) in X_FIRST:
                source, peer = tok.at[token_rows(by_x)], to_z
            else:
                source, peer = tok.at[token_rows(by_z)], to_x
        return slot_copy(4, s, source, tok.at[token_rows(s)], peer)

    def back_copy(s):
        return slot_copy(5, s, mixed_send.at[pl.ds(16 * s, 16)], mixed_recv.at[s], near_req(s))

    def each(first, last, action):
        for s in range(first, last):
            action(s)

    def start_all(phase, count, axis, source, target):
        def body(o, carry):
            remote(phase, o, axis, source, target).start()
            return carry

        lax.fori_loop(1, count, body, 0)

    def wait_recv_all(phase, count, axis, source, target):
        def body(o, carry):
            remote(phase, o, axis, source, target).wait_recv()
            return carry

        lax.fori_loop(1, count, body, 0)

    def wait_send_all(phase, count, axis, source, target):
        def body(o, carry):
            remote(phase, o, axis, source, target).wait_send()
            return carry

        lax.fori_loop(1, count, body, 0)

    eye = iota((128, 128), 0) == iota((128, 128), 1)

    def column(row):
        return jnp.sum(jnp.where(eye, row, 0.0), 1, keepdims=True)

    def wide_row(ref):
        return jnp.concatenate([ref[i : i + 1, :] for i in range(ref.shape[0])], 1)

    slots = slots_ref[...]
    owner = (slots * 43691) >> 17
    page = slots - owner * PAGES
    home = owner >> 7
    place = page * 128 + (owner & 127)
    home_f = home.astype(F32)
    place_f = place.astype(F32)
    home_row = jnp.concatenate([home_f[i : i + 1] for i in range(3)], 1)
    place_row = jnp.concatenate([place_f[i : i + 1] for i in range(3)], 1)
    home_col = jnp.concatenate([column(home_f[i : i + 1]) for i in range(3)], 0)
    place_col = jnp.concatenate([column(place_f[i : i + 1]) for i in range(3)], 0)
    home_hot = (home_row == iota((16, blocks), 0).astype(F32)).astype(F32).astype(BF16)
    order_row = home_row * 384.0 + place_row
    order_col = home_col * 384.0 + place_col
    before = (order_col < order_row).astype(F32)
    slot_row = jnp.sum(before, 0, keepdims=True) + 8.0 * home_row
    after = (order_row < order_col).astype(F32)
    slot_col = jnp.sum(after, 1, keepdims=True) + 8.0 * home_col
    rank = slot_col - PAD * home_col + 1.0
    place_rank = jnp.where(place_col == iota((blocks, blocks), 1).astype(F32), rank, 0.0)
    present = dot_nn(home_hot, place_rank.astype(BF16))
    pm_send[...] = jnp.zeros_like(pm_send)
    q_recv[...] = jnp.zeros_like(q_recv)
    part_recv[...] = jnp.zeros_like(part_recv)
    for j in range(PAGES):
        pm_send[:, j, :] = present[:, 128 * j : 128 * (j + 1)]

    pl.semaphore_wait(barrier, n_req + 3)
    presence = (0, n_req, "req", lambda peer: pm_send.at[peer], pm_recv.at[me])
    for o in FAR:
        remote(0, o, "req", presence[3], presence[4]).start()
    pm_recv[pl.ds(me, 1)] = pm_send[pl.ds(me, 1)]

    n_slot = n_req * PAD

    len_row = lens_ref[pl.ds(me, 1), :].astype(F32)
    len_col = column(len_row)
    lane = iota((rows, 256), 1)
    frequency = jnp.exp((lane & 31).astype(F32) * (-9.210340371976184 / 32.0))
    angles = len_col * frequency
    cosines = jnp.cos(angles)
    sines = jnp.sin(angles)
    upper = (lane & 63) >= 32
    for load in loads[:4]:
        load.wait()
    values = hid[...].astype(F32)
    scale = lax.rsqrt(jnp.mean(values * values, -1, keepdims=True) + 1e-05)
    normed = (values * scale * wide_row(gain_ref)).astype(BF16)
    qk = dot_nt(normed, wqkv[pl.ds(0, 256), :])
    value_new[...] = dot_nt(normed, wqkv[pl.ds(256, 64), :]).astype(BF16)
    swapped = jnp.where(upper, pltpu.roll(qk, 32, 1), pltpu.roll(qk, 224, 1))
    turned = qk * cosines + jnp.where(upper, swapped, -swapped) * sines
    turned = jnp.where(lane < 192, turned * 0.125, turned).astype(BF16)
    rotated[...] = turned

    wait_recv_all(*presence)
    held = pm_recv[...]
    base = (iota((16, 8, 128), 0) * PAD - 1).astype(F32)
    page_slot = jnp.sum(jnp.where(held > 0.0, held + base, 0.0), 0)
    page_row = jnp.concatenate([page_slot[j : j + 1] for j in range(PAGES)], 1)
    extended = []
    for j in range(PAGES):
        used = jnp.clip(len_col - 128.0 * j, 0.0, 128.0)
        extended.append(jnp.where(lane < 192, turned.astype(F32), used).astype(BF16))
    extended = jnp.concatenate(extended, 0)

    def z_rows(oz):
        z = (mz + oz) % 4
        return z, pl.ds(pl.multiple_of(z * 4 * PAD, 4 * PAD), 4 * PAD)

    def slot_rows(index):
        return pl.ds(pl.multiple_of(index * PAD, PAD), SHARE)

    queries = (1, n_req, "req", lambda peer: q_send.at[slot_rows(peer)], q_recv.at[slot_rows(me)])
    for oz in (2, 1, 3, 0):
        z, there = z_rows(oz)
        number = (iota((4 * PAD, blocks), 0) + z * 4 * PAD).astype(F32)
        pick = (number == page_row).astype(F32).astype(BF16)
        q_send[there, :] = dot_nn(pick, extended).astype(BF16)
        for ox in (2, 1, 3, 0):
            if (oz, ox) != (0, 0):
                remote(1, oz * 4 + ox, "req", queries[3], queries[4]).start()
    page_col = jnp.concatenate([column(page_slot[j : j + 1]) for j in range(PAGES)], 0)
    gather_t[...] = (iota((blocks, n_slot), 1).astype(F32) == page_col).astype(F32).astype(BF16)
    expert_row = iota((128, 16), 0)
    chosen = jnp.zeros((128, 16), F32)
    for k in range(8):
        chosen = chosen + (routes_ref[k : k + 1, :] == expert_row).astype(F32)
    eye_16 = (iota((16, 16), 0) == iota((16, 16), 1)).astype(F32).astype(BF16)
    mask_send[...] = dot_nt(eye_16, chosen.astype(BF16)).astype(BF16)
    mask_recv[0:16, :] = mask_send[...]
    loads[7].start()
    loads[8].start()
    loads[6].wait()
    share_w = remote(0, 0, "core", lambda peer: wout, wout_peer)
    share_w.start()
    q_recv[slot_rows(me), :] = q_send[slot_rows(me), :]
    place_slot = (slot_col == iota((blocks, n_slot), 1).astype(F32)).astype(F32).astype(BF16)
    slot_place[...] = (iota((n_slot, blocks), 0).astype(F32) == slot_row).astype(F32).astype(BF16)
    wait_recv_all(*queries)
    each(1, n_req, lambda s: mask_copy(s).start())
    arrived = dot_nn(place_slot, q_recv[...])
    zeros = jnp.zeros((blocks, HD), BF16)
    for q in range(3):
        head = arrived[:, HD * q : HD * (q + 1)].astype(BF16)
        q6[q] = jnp.concatenate([head, zeros], 1)
        q6[q + 3] = jnp.concatenate([zeros, head], 1)
    limit = arrived[:, 192:256]
    thr[...] = jnp.concatenate([limit, limit], 1)

    loads[4].wait()
    loads[5].wait()
    wide_r, wide_c = iota((96, 256), 0), iota((96, 256), 1)
    position = jnp.where((wide_r & 15) == (wide_c & 15), 2 * (wide_c >> 4), 1 << 20).astype(F32)
    stat_lane = iota((16, HD), 1)

    def some_groups(step, carry):
        at = [pl.ds(pl.multiple_of((step * 8 + k) * 16, 16), 16) for k in range(8)]
        scores = []
        for here in at:
            query = q6[:, here, :].reshape(96, 128)
            bound = thr[here, :]
            bound = jnp.concatenate([bound] * 3 + [bound - 1.0] * 3, 0)
            bound = jnp.concatenate([bound, bound], 1)
            mine = []
            for c in range(4):
                keys = jnp.concatenate(
                    [kbuf[here, 128 * i : 128 * (i + 1)] for i in range(16 * c, 16 * c + 16)], 0
                )
                mine.append(jnp.where(position < bound - 32.0 * c, dot_nt(query, keys), LOW))
            scores.append(mine)
        tops, weights, totals = [], [], []
        for mine in scores:
            top = jnp.maximum(jnp.maximum(mine[0], mine[1]), jnp.maximum(mine[2], mine[3]))
            top = jnp.max(top, 1, keepdims=True)
            top = jnp.maximum(jnp.maximum(top[:48], top[48:]), -1e29)
            top_2 = jnp.concatenate([top, top], 0)
            these = [jnp.exp(s - top_2) for s in mine]
            total = jnp.sum((these[0] + these[1]) + (these[2] + these[3]), 1, keepdims=True)
            tops.append(top)
            weights.append([w.astype(BF16) for w in these])
            totals.append(total[:48] + total[48:])
        for here, top, these, total in zip(at, tops, weights, totals):
            numer = jnp.zeros((96, 128), F32)
            for c in range(4):
                vals = jnp.concatenate(
                    [vbuf[here, 128 * i : 128 * (i + 1)] for i in range(16 * c, 16 * c + 16)], 0
                )
                numer = numer + dot_nn(these[c], vals)
            numer = numer[:48, :HD] + numer[48:, HD:]
            some = total > 0.0
            safe = jnp.where(some, total, 1.0)
            numer = numer / safe
            lse = jnp.where(some, top + jnp.log(safe), LOW)
            pieces = [numer[16 * q : 16 * (q + 1)] for q in range(3)]
            stats = jnp.zeros((16, HD), F32)
            for q in range(3):
                for t, term in enumerate(split_3(lse[16 * q : 16 * (q + 1)])):
                    stats = jnp.where(stat_lane == 16 * t + q, term, stats)
            part[here, :] = jnp.concatenate(pieces + [stats], 1).astype(BF16)
        return carry

    lax.fori_loop(0, blocks // (16 * 8), some_groups, 0)

    partials = (
        2, n_req, "req", lambda peer: part_send.at[slot_rows(peer)], part_recv.at[slot_rows(me)],
    )
    for oz in (2, 1, 3, 0):
        z, there = z_rows(oz)
        part_send[there, :] = dot_nn(slot_place[there, :], part[...]).astype(BF16)
        for ox in (2, 1, 3, 0):
            if (oz, ox) != (0, 0):
                remote(2, oz * 4 + ox, "req", partials[3], partials[4]).start()
    part_recv[slot_rows(me), :] = part_send[slot_rows(me), :]
    own_q = rotated[...].astype(F32)
    own_k = own_q[:, 192:256]
    own_v = value_new[...].astype(F32)
    own_score = [
        jnp.broadcast_to(
            jnp.sum(own_q[:, HD * q : HD * (q + 1)] * own_k, 1, keepdims=True), (rows, HD)
        )
        for q in range(3)
    ]
    own_score = jnp.concatenate(own_score + [jnp.zeros((rows, HD), F32)], 1)
    own_v = jnp.concatenate([own_v] * 4, 1)
    spread_r, spread_c = iota((HD, 256), 0), iota((HD, 256), 1)
    spread = ((spread_r & 15) == (spread_c >> 6)) & (spread_r < 48) & (spread_c < 192)
    spread = spread.astype(F32).astype(BF16)
    wait_recv_all(*partials)
    pages = dot_nn(gather_t[...], part_recv[...])
    lses = dot_nn(pages[:, 192:256].astype(BF16), spread)
    lses = [own_score] + [lses[128 * j : 128 * (j + 1)] for j in range(PAGES)]
    outs = [own_v] + [pages[128 * j : 128 * (j + 1)] for j in range(PAGES)]
    peak = jnp.maximum(jnp.maximum(lses[0], lses[1]), jnp.maximum(lses[2], lses[3]))
    shares = [jnp.exp(value - peak) for value in lses]
    whole = (shares[0] + shares[1]) + (shares[2] + shares[3])
    summed = shares[0] * outs[0] + shares[1] * outs[1]
    summed = summed + shares[2] * outs[2] + shares[3] * outs[3]
    attended = summed / whole
    attended = jnp.where(lane < 192, attended, 0.0).astype(BF16)
    att[...] = attended.reshape(4, 2, 16, 256)
    swap = remote(3, 0, "core", lambda peer: att.at[:, 1 - core], att_peer)
    swap.start()

    own_rows = att[:, pl.ds(core, 1)].reshape(64, 256)[:, :192]
    def sum_copy(h, o):
        peer = (kv + 2 * o) % n_kv
        lanes = pl.ds(half * h, half)
        return pltpu.make_async_remote_copy(
            src_ref=proj.at[peer // 2, :, lanes], dst_ref=proj_recv.at[o, :, lanes],
            send_sem=send_sem.at[3, 4 * h + o], recv_sem=recv_sem.at[3, 4 * h + o],
            device_id={"kv": peer}, device_id_type=MESH,
        )

    own_part = [dot_nn(own_rows, wout[:, n : n + half]) for n in range(0, model, half)]
    share_w.wait_recv()
    swap.wait_recv()
    peer_rows = att_peer[...].reshape(64, 256)[:, :192]
    for h in range(2):
        lanes = pl.ds(half * h, half)
        both = own_part[h] + dot_nn(peer_rows, wout_peer[:, lanes])
        proj[:, :, lanes] = both.astype(BF16).reshape(4, 16, half)
        for o in (2, 1, 3):
            sum_copy(h, o).start()
    own_proj = proj[pl.ds(kv // 2, 1)].reshape(16, model).astype(F32)
    for h in range(2):
        for o in range(1, 4):
            sum_copy(h, o).wait_recv()
    after_attn = hid[token_rows(kv), :].astype(F32)
    total = own_proj
    for k in range(1, 4):
        total = total + proj_recv[k].astype(F32)
    after_attn = after_attn + total
    scale = lax.rsqrt(jnp.mean(after_attn * after_attn, -1, keepdims=True) + 1e-05)
    moe_in = (after_attn * scale * wide_row(moe_gain_ref)).astype(BF16)
    tok_send[...] = moe_in
    each(1, DIRECT, lambda s: token_copy(s).start())
    tok[0:16, :] = tok_send[...]
    for s, onward in ((1, [(1, 2), (3, 2)]), (2, [(2, 1), (2, 3), (2, 2)])):
        token_copy(s).wait_recv()
        for place in onward:
            token_copy(ORDER.index(place)).start()
    loads[7].wait()
    loads[8].wait()
    each(1, n_req, lambda s: mask_copy(s).wait_recv())
    for first, last in CHUNKS:
        each(max(first, 3), last, lambda s: token_copy(s).wait_recv())
        count = 16 * (last - first)
        here = pl.ds(16 * first, count)
        gate_lane = iota((count, 128), 1)
        inputs = tok[here, :]
        logits = jnp.concatenate([dot_nt(inputs, router_ref[...])] * 4, 1)
        logits = jnp.where(mask_recv[here, :].astype(F32) > 0.0, logits, LOW)
        gates = jnp.exp(logits - jnp.max(logits, 1, keepdims=True))
        gates = gates / jnp.sum(gates, 1, keepdims=True)
        acts, gains = [], []
        for e in range(2):
            gains.append(jnp.sum(jnp.where(gate_lane == 2 * me + e, gates, 0.0), 1, keepdims=True))
            these = []
            for f in range(0, FFE, 256):
                gate = dot_nn(inputs, up[e, :, f : f + 256])
                lift = dot_nn(inputs, up[e, :, FFE + f : FFE + f + 256])
                these.append((gate * jax.nn.sigmoid(gate) * lift).astype(BF16))
            acts.append(jnp.concatenate(these, 1))
        for h in range(2):
            for n in range(half * h, half * (h + 1), 256):
                made = [
                    dot_nn(acts[e], down[e, :, n : n + 256]).astype(BF16).astype(F32) * gains[e]
                    for e in range(2)
                ]
                mixed_send[here, n : n + 256] = (made[0] + made[1]).astype(BF16)
            if first < SPLIT and h == 1:
                each(max(first, 1), last, lambda s: back_copy(s).start())
            elif first >= SPLIT:
                each(first, last, lambda s: half_back(s, h).start())

    each(1, n_req, lambda s: mask_copy(s).wait_send())
    each(1, n_req, lambda s: token_copy(s).wait_send())
    each(1, n_req, lambda s: [copy.wait_send() for copy in back_copies(s)])
    share_w.wait_send()
    swap.wait_send()
    for h in range(2):
        for o in range(1, 4):
            sum_copy(h, o).wait_send()
    for exchange in (presence, queries, partials):
        wait_send_all(*exchange)
    result = mixed_send[0:16, :].astype(F32)
    for d in range(1, n_req):
        for copy in back_copies(d):
            copy.wait_recv()
        result = result + mixed_recv[d].astype(F32)
    out_ref[...] = (after_attn + result).astype(BF16)


def shards(
    hidden_in, attn_gain, w_query, w_key, w_value, w_out, k_cache, v_cache, cache_len, block_slot,
    moe_gain, w_router, w_gate_up, w_down, routes,
):
    any_spec = pl.BlockSpec(memory_space=pl.ANY)
    vmem = pl.BlockSpec(memory_space=pltpu.VMEM)
    blocks = k_cache.shape[0]
    model = hidden_in.shape[1]
    rows = hidden_in.shape[0]
    n_slot = 16 * PAD
    scratch = [
        ((rows, model), BF16), ((320, model), BF16), ((192, model), BF16),
        ((blocks, 8192), BF16), ((blocks, 8192), BF16),
        (w_gate_up.shape, BF16), (w_down.shape, BF16),
        ((16, 8, 128), F32), ((16, 8, 128), F32),
        ((n_slot, 256), BF16), ((n_slot, 256), BF16),
        ((6, blocks, 128), BF16), ((blocks, 128), F32),
        ((blocks, 256), BF16), ((n_slot, 256), BF16), ((n_slot, 256), BF16),
        ((blocks, n_slot), BF16),
        ((rows, 256), BF16), ((rows, HD), BF16), ((4, 16, model), BF16), ((4, 16, model), BF16),
        ((4, 2, 16, 256), BF16), ((4, 16, 256), BF16), ((192, model), BF16),
        ((16, 128), BF16), ((256, 128), BF16), ((n_slot, blocks), BF16),
        ((16, model), BF16), ((256, model), BF16),
        ((256, model), BF16), ((16, 16, model), BF16),
    ]
    return pl.pallas_call(
        kernel,
        out_shape=jax.ShapeDtypeStruct((16, model), BF16),
        in_specs=[any_spec] * 15,
        out_specs=vmem,
        scratch_shapes=[
            pltpu.VMEM((model // 128, 128), F32), pltpu.VMEM((16, 128), jnp.int32),
            pltpu.VMEM((3, 128), jnp.int32), pltpu.VMEM((model // 128, 128), F32),
            pltpu.VMEM((32, model), BF16), pltpu.VMEM((8, 16), jnp.int32),
        ]
        + [pltpu.VMEM(shape, dtype) for shape, dtype in scratch]
        + [
            pltpu.SemaphoreType.DMA((15,)),
            pltpu.SemaphoreType.DMA((8, 16)),
            pltpu.SemaphoreType.DMA((8, 16)),
        ],
        compiler_params=pltpu.CompilerParams(
            collective_id=0, has_side_effects=True, vmem_limit_bytes=56 << 20
        ),
    )(
        hidden_in, attn_gain.reshape(model // 128, 128), w_query, w_key, w_value, w_out,
        k_cache.reshape(blocks, 8192), v_cache.reshape(blocks, 8192),
        cache_len.reshape(16, 128), block_slot.reshape(3, 128),
        moe_gain.reshape(model // 128, 128), w_router.T, w_gate_up, w_down, routes.T,
    )


def solution(mesh):
    placed = (
        P("req", None),
        P(),
        P("kv", None),
        P("kv", None),
        P("kv", None),
        P("kv", None),
        P("req", "kv", None),
        P("req", "kv", None),
        P(),
        P("req"),
        P(),
        P(),
        P("req", None, None),
        P("req", None, None),
        P(("req", "kv"), None),
    )
    return jax.shard_map(
        shards, mesh=mesh, in_specs=placed, out_specs=P(("req", "kv"), None), check_vma=False
    )
```
